32 devices in a mesh: dp: 2 (over y), seq: 16 (over z, x, core).
Axes of the slice: x: 2, y: 2, z: 4, core: 2. Of those that a mesh axis runs over, the one named last changes fastest.
Arguments:
- tokens: bfloat16 [4, 2048, 768], P('dp', 'seq'), may hold values from -6 to 6
- segments: int32 [4, 2048], P('dp', 'seq'), may hold values from 0 to 1, never falling along the last dimension, each value on 1 to 2000 neighbouring positions
- qkv_weight: bfloat16 [768, 2304], P(('dp', 'seq')), may hold values from -0.21875 to 0.21875
- out_weight: bfloat16 [768, 768], P(('dp', 'seq')), may hold values from -4 to 4
- up_weight: bfloat16 [768, 3072], P(('dp', 'seq')), may hold values from -0.21875 to 0.21875
- down_weight: bfloat16 [3072, 768], P(('dp', 'seq')), may hold values from -0.109375 to 0.109375
- query_bias: bfloat16 [768], P(('dp', 'seq')), may hold values from -3 to 3
- value_bias: bfloat16 [768], P(('dp', 'seq')), may hold values from -3 to 3
- out_bias: bfloat16 [768], P(('dp', 'seq')), may hold values from -3 to 3
- first_gain: bfloat16 [768], P(('dp', 'seq')), may hold values from 0.099609375 to 1.8984375
- first_shift: bfloat16 [768], P(('dp', 'seq')), may hold values from -3 to 3
- up_bias: bfloat16 [3072], P(('dp', 'seq')), may hold values from -3 to 3
- down_bias: bfloat16 [768], P(('dp', 'seq')), may hold values from -3 to 3
- second_gain: bfloat16 [768], P(('dp', 'seq')), may hold values from 0.099609375 to 1.8984375
- second_shift: bfloat16 [768], P(('dp', 'seq')), may hold values from -3 to 3
- cotangent: bfloat16 [4, 2048, 768], P('dp', 'seq'), may hold values from -6 to 6
Outputs:
- layer_output: bfloat16 [4, 2048, 768], P('dp', 'seq')
- input_grad: bfloat16 [4, 2048, 768], P('dp', 'seq')
- grad_qkv_weight: float32 [768, 2304], P(('dp', 'seq'))
- grad_out_weight: float32 [768, 768], P(('dp', 'seq'))
- grad_up_weight: float32 [768, 3072], P(('dp', 'seq'))
- grad_down_weight: float32 [3072, 768], P(('dp', 'seq'))
- grad_query_bias: float32 [768], P(('dp', 'seq'))
- grad_value_bias: float32 [768], P(('dp', 'seq'))
- grad_out_bias: float32 [768], P(('dp', 'seq'))
- grad_first_gain: float32 [768], P(('dp', 'seq'))
- grad_first_shift: float32 [768], P(('dp', 'seq'))
- grad_up_bias: float32 [3072], P(('dp', 'seq'))
- grad_down_bias: float32 [768], P(('dp', 'seq'))
- grad_second_gain: float32 [768], P(('dp', 'seq'))
- grad_second_shift: float32 [768], P(('dp', 'seq'))
The draws below stay inside these ranges and needn't reach their ends.
Inputs may be any that keep to these rules, and one draw needn't show every extreme that they name: `segments`: in each sequence segment numbers never fall from one token to the next, every number up to 1 appears, each document holds at most 2000 tokens.
All inputs are finite; a program needn't handle non-finite values.
Results may differ from the reference program's by a relative error of at most 0.017.
Values may be sent and summed in bfloat16 or wider, within the bound.
No kernel may reach another device: no remote copies, remote signals or barrier semaphores. Data moves between devices by JAX's collectives and lax.ppermute only.
A program may use at most 320 MiB of HBM per device.

```python
import math
import jax
import jax.numpy as jnp
import numpy as np
from jax import lax

D = 768
HEADS = 12
HEAD_DIM = 64
FF = 3072
DOC_MOST = 2000
SEQS = 4
LEN = 2048
DOCS = 2


def level_of(own_key, extent, shards, low, largest):
    gain, own = 1.0, jax.random.fold_in(own_key, 6)
    for axis_at, shards_of in shards:
        steps = jnp.exp(jax.random.uniform(jax.random.fold_in(own, axis_at), (shards_of,), jnp.float32, low / len(shards), largest / len(shards)))
        gain = gain * jnp.repeat(steps, extent[axis_at] // shards_of).reshape([-1 if axis == axis_at else 1 for axis in range(len(extent))])
    return gain


def length_profile(count, total, bound, lean):
    weights = [(1 << 20) // math.isqrt(standing ** lean) + 1 for standing in range(2, count + 1)]
    surplus, holding = total - bound - (count - 1), [1] * (count - 1)
    while surplus > 0:
        free = [i for i in range(count - 1) if holding[i] < bound]
        mass, remaining = sum([weights[i] for i in free]), surplus
        for i in free:
            more = min(bound - holding[i], max(1, remaining * weights[i] // mass), surplus)
            holding[i] = holding[i] + more
            surplus = surplus - more
    return np.array([bound] + holding)


def ragged(rng, count, total, most, lean):
    if count == 2:
        one = jax.random.randint(rng, (), max(1, total - most), min(most, total - 1) + 1)
        return jnp.stack([one, total - one])
    lengths = jnp.asarray(length_profile(count, total, most, lean), jnp.int32)
    pairs = (count - 1) // 2
    giver, sink = lengths[1:1 + 2 * pairs:2], lengths[2:2 + 2 * pairs:2]
    slack = jnp.minimum(giver - 1, most - sink)
    shifted = jax.random.randint(jax.random.fold_in(rng, 1), (pairs,), 0, 1 << 20) % (slack + 1)
    lengths = lengths.at[1:1 + 2 * pairs:2].set(giver - shifted).at[2:2 + 2 * pairs:2].set(sink + shifted)
    return lengths[jax.random.permutation(jax.random.fold_in(rng, 2), count)]


def bell_draw(stream_key, shape, deviation, most, split=(), held_as=jnp.bfloat16):
    level = level_of(stream_key, shape, split, -0.22, 0.18) if split else 1.0
    values = jax.random.normal(stream_key, shape, jnp.float32) * deviation * level
    return jnp.minimum(jnp.maximum(values, -most), most).astype(held_as)


def setup_inputs(seed: int = 0) -> dict:
    keys = jax.random.split(jax.random.key(seed), 17)
    tokens = bell_draw(keys[0], (SEQS, LEN, D), 1.0, 6.0, ((0, 2), (1, 16)))
    segments = jax.vmap(lambda own: jnp.searchsorted(jnp.cumsum(ragged(own, DOCS, LEN, DOC_MOST, 2)), jnp.arange(LEN), side="right"))(jax.random.split(keys[1], SEQS)).reshape((SEQS, LEN)).astype(jnp.int32)
    qkv_weight = bell_draw(keys[2], (D, 3 * D), D ** -0.5, 0.21875, ((0, 32),))
    out_weight = bell_draw(keys[3], (D, D), 2 ** -0.5, 4.0, ((0, 32),))
    up_weight = bell_draw(keys[4], (D, FF), D ** -0.5, 0.21875, ((0, 32),))
    down_weight = bell_draw(keys[5], (FF, D), FF ** -0.5, 0.109375, ((0, 32),))
    query_bias = bell_draw(keys[6], (D,), 0.5, 3.0, ((0, 32),))
    value_bias = bell_draw(keys[7], (D,), 0.5, 3.0, ((0, 32),))
    out_bias = bell_draw(keys[8], (D,), 0.5, 3.0, ((0, 32),))
    first_gain = jnp.clip(1.0 + 0.18 * jax.random.normal(keys[9], (D,), jnp.float32), 0.099609375, 1.8984375).astype(jnp.bfloat16)
    first_shift = bell_draw(keys[10], (D,), 0.5, 3.0, ((0, 32),))
    up_bias = bell_draw(keys[11], (FF,), 0.5, 3.0, ((0, 32),))
    down_bias = bell_draw(keys[12], (D,), 0.5, 3.0, ((0, 32),))
    second_gain = jnp.clip(1.0 + 0.18 * jax.random.normal(keys[13], (D,), jnp.float32), 0.099609375, 1.8984375).astype(jnp.bfloat16)
    second_shift = bell_draw(keys[14], (D,), 0.5, 3.0, ((0, 32),))
    cotangent = bell_draw(keys[15], (SEQS, LEN, D), 1.0, 6.0, ((0, 2), (1, 16)))
    return dict(tokens=tokens, segments=segments, qkv_weight=qkv_weight, out_weight=out_weight, up_weight=up_weight, down_weight=down_weight, query_bias=query_bias, value_bias=value_bias, out_bias=out_bias, first_gain=first_gain, first_shift=first_shift, up_bias=up_bias, down_bias=down_bias, second_gain=second_gain, second_shift=second_shift, cotangent=cotangent)


@jax.custom_vjp
def low(v):
    return lax.optimization_barrier(v.astype(jnp.bfloat16)).astype(jnp.float32)

@jax.custom_vjp
def low_back(v):
    return v

def low_keep(v):
    return (low(v), None)

def low_pass(kept, grad):
    return (grad,)

def back_keep(v):
    return (v, None)

def back_low(kept, grad):
    return (low(grad),)
low.defvjp(low_keep, low_pass)
low_back.defvjp(back_keep, back_low)
EPS = 1e-12
HIGHEST = lax.Precision.HIGHEST

def norm_layer(summed, gain_row, shift_row):
    average = lax.optimization_barrier(jnp.mean(summed, axis=-1, keepdims=True))
    centred = summed - average
    variance = lax.optimization_barrier(jnp.mean(centred * centred, axis=-1, keepdims=True))
    return centred * lax.rsqrt(variance + EPS) * gain_row + shift_row

def attend(query_rows, key_rows, value_rows, segment_row):
    length = query_rows.shape[0]
    block_rows = math.gcd(length, 512)
    block_count = length // block_rows
    query_blocks = query_rows.reshape(block_count, block_rows, HEADS, HEAD_DIM)
    segment_blocks = segment_row.reshape(block_count, block_rows)
    key_heads = key_rows.reshape(length, HEADS, HEAD_DIM)
    value_heads = value_rows.reshape(length, HEADS, HEAD_DIM)

    def one_block(inputs_pair):
        query_block, segment_block = inputs_pair
        scores = jnp.einsum('qhd,khd->hqk', query_block, key_heads, precision=HIGHEST) * 0.125
        scores = low_back(scores)
        allowed = segment_block[:, None] == segment_row[None, :]
        scores = jnp.where(allowed[None], scores, -jnp.inf)
        weights_low = low(jax.nn.softmax(scores, axis=-1))
        return jnp.einsum('hqk,khd->qhd', weights_low, value_heads, precision=HIGHEST)
    result = lax.map(jax.checkpoint(one_block), (query_blocks, segment_blocks))
    return result.reshape(length, D)

def layer(tokens_f, segment_row, qkv_weight, out_weight, up_weight, down_weight, query_bias, value_bias, out_bias, first_gain, first_shift, up_bias, down_bias, second_gain, second_shift):
    merged = jnp.dot(tokens_f, qkv_weight, precision=HIGHEST)
    query = low(low_back(merged[:, :D] + query_bias))
    key_rows = low(low_back(merged[:, D:2 * D]))
    values = low(low_back(merged[:, 2 * D:] + value_bias))
    attended = low(low_back(attend(query, key_rows, values, segment_row)))
    branch = low_back(jnp.dot(attended, out_weight, precision=HIGHEST) + out_bias)
    hidden = norm_layer(tokens_f + branch, first_gain, first_shift)
    inner_rows = low_back(jnp.dot(low(hidden), up_weight, precision=HIGHEST) + up_bias)
    activated = low(jax.nn.gelu(inner_rows, approximate=False))
    second = low_back(jnp.dot(activated, down_weight, precision=HIGHEST) + down_bias)
    return norm_layer(hidden + second, second_gain, second_shift)

def reference(tokens, segments, qkv_weight, out_weight, up_weight, down_weight, query_bias, value_bias, out_bias, first_gain, first_shift, up_bias, down_bias, second_gain, second_shift, cotangent):
    params = tuple((item.astype(jnp.float32) for item in (qkv_weight, out_weight, up_weight, down_weight, query_bias, value_bias, out_bias, first_gain, first_shift, up_bias, down_bias, second_gain, second_shift)))

    def step(totals, inputs_seq):
        seq_tokens, seq_segments, seq_cotangent = inputs_seq

        def apply_layer(tokens_f, *weights):
            return layer(tokens_f, seq_segments, *weights)
        output, pullback = jax.vjp(apply_layer, seq_tokens.astype(jnp.float32), *params)
        grads = pullback(seq_cotangent.astype(jnp.float32))
        totals = tuple((total_item + grad_item for total_item, grad_item in zip(totals, grads[1:])))
        return (totals, (output.astype(jnp.bfloat16), grads[0].astype(jnp.bfloat16)))
    zeros_init = tuple((jnp.zeros(item.shape, jnp.float32) for item in params))
    totals, (outputs, input_grads) = lax.scan(step, zeros_init, (tokens, segments, cotangent))
    return (outputs, input_grads, totals[0], totals[1], totals[2], totals[3], totals[4], totals[5], totals[6], totals[7], totals[8], totals[9], totals[10], totals[11], totals[12])
```

```python
import jax
import jax.numpy as jnp
from jax import lax
from jax.experimental import pallas as pl
from jax.experimental.pallas import tpu as pltpu
from jax.sharding import PartitionSpec as P

HEADS = 12
HEAD_DIM = 64
FF = 3072
DOC_MOST = 2000


EPS = 1e-12
NEGATIVE = -1e30


def norm_layer(summed, gain_row, shift_row):
    average = jnp.mean(summed, axis=-1, keepdims=True)
    centred = summed - average
    variance = jnp.mean(centred * centred, axis=-1, keepdims=True)
    return centred * lax.rsqrt(variance + EPS) * gain_row + shift_row


def exact_gelu(inner_rows):
    return jax.nn.gelu(inner_rows, approximate=False)


def same_value(state_pair):
    return state_pair


def head_split(matrix):
    return matrix.reshape(matrix.shape[0], HEADS, HEAD_DIM)


def block_scores(query_heads, key_rows):
    return (
        jnp.einsum(
            "qhd,khd->hqk", query_heads, head_split(key_rows), preferred_element_type=jnp.float32
        )
        * 0.125
    )


def probabilities(query_heads, key_stack, block_index, allowed, log_total):
    scores = block_scores(query_heads, key_stack[block_index, :, : HEADS * HEAD_DIM])
    return jnp.where(allowed[None], jnp.exp(scores - log_total[:, :, None]), 0.0)


def block_mask(query_segment, key_segments, block_index):
    return query_segment[:, None] == key_segments[block_index][None, :]


def log_totals(query_heads, key_stack, key_segments, query_segment):
    row_count = query_heads.shape[0]

    def log_visit(block_index, carry_state):
        allowed = block_mask(query_segment, key_segments, block_index)

        def log_compute(state_pair):
            top_now, total_now = state_pair
            scores = jnp.where(
                allowed[None],
                block_scores(query_heads, key_stack[block_index, :, : HEADS * HEAD_DIM]),
                NEGATIVE,
            )
            top_new = jnp.maximum(top_now, jnp.max(scores, axis=-1))
            expon_rows = jnp.where(allowed[None], jnp.exp(scores - top_new[:, :, None]), 0.0)
            return (top_new, total_now * jnp.exp(top_now - top_new) + jnp.sum(expon_rows, axis=-1))

        return lax.cond(jnp.any(allowed), log_compute, same_value, carry_state)

    initial = (
        jnp.full((HEADS, row_count), NEGATIVE, jnp.float32),
        jnp.zeros((HEADS, row_count), jnp.float32),
    )
    top_final, total_final = lax.fori_loop(0, key_stack.shape[0], log_visit, initial)
    return top_final + jnp.log(total_final)


def attend_values(query_heads, key_stack, key_segments, query_segment, log_total):
    model_width = HEADS * HEAD_DIM

    def attend_visit(block_index, running):
        allowed = block_mask(query_segment, key_segments, block_index)

        def attend_compute(running_in):
            main_sum, rest_sum = running_in
            weights_block = probabilities(query_heads, key_stack, block_index, allowed, log_total)
            weights_low = weights_block.astype(jnp.bfloat16)
            weights_rest = (weights_block - weights_low.astype(jnp.float32)).astype(jnp.bfloat16)
            value_heads = head_split(key_stack[block_index, :, model_width:])
            main_new = main_sum + jnp.einsum(
                "hqk,khd->qhd", weights_low, value_heads, preferred_element_type=jnp.float32
            )
            rest_new = rest_sum + jnp.einsum(
                "hqk,khd->qhd", weights_rest, value_heads, preferred_element_type=jnp.float32
            )
            return (main_new, rest_new)

        return lax.cond(jnp.any(allowed), attend_compute, same_value, running)

    zero_heads = jnp.zeros(query_heads.shape, jnp.float32)
    main_sum, rest_sum = lax.fori_loop(
        0, key_stack.shape[0], attend_visit, (zero_heads, zero_heads)
    )
    return (main_sum.reshape(query_heads.shape[0], model_width), main_sum + rest_sum)


def attention_back(
    query_heads, grad_heads, key_stack, key_segments, query_segment, log_total, exact_heads
):
    model_width = HEADS * HEAD_DIM
    row_count = query_heads.shape[0]
    delta_rows = jnp.einsum("qhd,qhd->hq", grad_heads.astype(jnp.float32), exact_heads)

    def grad_visit(block_index, carry_state):
        allowed = block_mask(query_segment, key_segments, block_index)

        def grad_compute(state_pair):
            grad_query_in, contrib_in = state_pair
            weights_block = probabilities(query_heads, key_stack, block_index, allowed, log_total)
            key_heads = head_split(key_stack[block_index, :, :model_width])
            value_heads = head_split(key_stack[block_index, :, model_width:])
            grad_probs = jnp.einsum(
                "qhd,khd->hqk", grad_heads, value_heads, preferred_element_type=jnp.float32
            )
            grad_scores = (weights_block * (grad_probs - delta_rows[:, :, None])).astype(
                jnp.bfloat16
            )
            grad_query_new = grad_query_in + jnp.einsum(
                "hqk,khd->qhd", grad_scores, key_heads, preferred_element_type=jnp.float32
            )
            grad_keys = (
                jnp.einsum(
                    "hqk,qhd->khd", grad_scores, query_heads, preferred_element_type=jnp.float32
                )
                * 0.125
            )
            grad_values = jnp.einsum(
                "hqk,qhd->khd",
                weights_block.astype(jnp.bfloat16),
                grad_heads,
                preferred_element_type=jnp.float32,
            )
            joined = jnp.concatenate(
                [
                    grad_keys.reshape(row_count, model_width),
                    grad_values.reshape(row_count, model_width),
                ],
                axis=1,
            )
            return (
                grad_query_new,
                lax.dynamic_update_index_in_dim(contrib_in, joined, block_index, 0),
            )

        return lax.cond(jnp.any(allowed), grad_compute, same_value, carry_state)

    initial = (
        jnp.zeros(query_heads.shape, jnp.float32),
        jnp.zeros((key_stack.shape[0], row_count, 2 * model_width), jnp.float32),
    )
    grad_query, contrib = lax.fori_loop(0, key_stack.shape[0], grad_visit, initial)
    return ((grad_query * 0.125).reshape(row_count, model_width), contrib)


def weight_grad(left_rows, right_rows):
    return jnp.einsum("rk,rn->kn", left_rows, right_rows, preferred_element_type=jnp.float32)


def data_grad(grad_rows, weight_full):
    return jnp.einsum("rn,kn->rk", grad_rows, weight_full, preferred_element_type=jnp.float32)


def column_sum(rows_low):
    return jnp.sum(rows_low.astype(jnp.float32), axis=0)


def general_local(
    tokens,
    segments,
    qkv_weight,
    out_weight,
    up_weight,
    down_weight,
    query_bias,
    value_bias,
    out_bias,
    first_gain,
    first_shift,
    up_bias,
    down_bias,
    second_gain,
    second_shift,
    cotangent,
):
    batch_count, row_count, model_width = tokens.shape
    seq_count = lax.axis_size("seq")
    reach = min((DOC_MOST + row_count - 2) // row_count, seq_count - 1)
    window = 2 * reach + 1
    position = lax.axis_index("seq")
    every_segment = lax.all_gather(segments, "seq", axis=1, tiled=True)
    padded_segment = jnp.pad(
        every_segment, ((0, 0), (reach * row_count, reach * row_count)), constant_values=-1
    )
    totals = [
        jnp.zeros((model_width, 3 * model_width), jnp.float32),
        jnp.zeros((model_width, model_width), jnp.float32),
        jnp.zeros((model_width, FF), jnp.float32),
        jnp.zeros((FF, model_width), jnp.float32),
        jnp.zeros((model_width,), jnp.float32),
        jnp.zeros((model_width,), jnp.float32),
        jnp.zeros((model_width,), jnp.float32),
        jnp.zeros((model_width,), jnp.float32),
        jnp.zeros((model_width,), jnp.float32),
        jnp.zeros((FF,), jnp.float32),
        jnp.zeros((model_width,), jnp.float32),
        jnp.zeros((model_width,), jnp.float32),
        jnp.zeros((model_width,), jnp.float32),
    ]
    outputs = []
    input_grads = []
    for micro in range(batch_count):
        weights_now = (
            lax.all_gather(qkv_weight, ("dp", "seq"), axis=0, tiled=True),
            lax.all_gather(out_weight, ("dp", "seq"), axis=0, tiled=True),
            lax.all_gather(up_weight, ("dp", "seq"), axis=0, tiled=True),
            lax.all_gather(down_weight, ("dp", "seq"), axis=0, tiled=True),
            lax.all_gather(query_bias, ("dp", "seq"), axis=0, tiled=True),
            lax.all_gather(value_bias, ("dp", "seq"), axis=0, tiled=True),
            lax.all_gather(out_bias, ("dp", "seq"), axis=0, tiled=True),
            lax.all_gather(first_gain, ("dp", "seq"), axis=0, tiled=True),
            lax.all_gather(first_shift, ("dp", "seq"), axis=0, tiled=True),
            lax.all_gather(up_bias, ("dp", "seq"), axis=0, tiled=True),
            lax.all_gather(down_bias, ("dp", "seq"), axis=0, tiled=True),
            lax.all_gather(second_gain, ("dp", "seq"), axis=0, tiled=True),
            lax.all_gather(second_shift, ("dp", "seq"), axis=0, tiled=True),
        )
        (
            qkv_full,
            out_full,
            up_full,
            down_full,
            query_b,
            value_b,
            out_b,
            first_g,
            first_s,
            up_b,
            down_b,
            second_g,
            second_s,
        ) = weights_now
        inputs = tokens[micro]
        merged = jnp.dot(inputs, qkv_full, preferred_element_type=jnp.float32)
        query = (merged[:, :model_width] + query_b.astype(jnp.float32)).astype(jnp.bfloat16)
        keys_now = merged[:, model_width : 2 * model_width].astype(jnp.bfloat16)
        values_now = (merged[:, 2 * model_width :] + value_b.astype(jnp.float32)).astype(
            jnp.bfloat16
        )
        whole_keys = lax.all_gather(
            jnp.concatenate([keys_now, values_now], axis=1), "seq", axis=0, tiled=True
        )
        padded = jnp.pad(whole_keys, ((reach * row_count, reach * row_count), (0, 0)))
        picked = lax.dynamic_slice_in_dim(padded, position * row_count, window * row_count, 0)
        key_stack = picked.reshape(window, row_count, 2 * model_width)
        key_segments = lax.dynamic_slice_in_dim(
            padded_segment[micro], position * row_count, window * row_count, 0
        ).reshape(window, row_count)
        query_segment = segments[micro]
        query_heads = head_split(query)
        log_total = log_totals(query_heads, key_stack, key_segments, query_segment)
        attended_f, exact_heads = attend_values(
            query_heads, key_stack, key_segments, query_segment, log_total
        )
        attended = attended_f.astype(jnp.bfloat16)
        branch = jnp.dot(attended, out_full, preferred_element_type=jnp.float32) + out_b.astype(
            jnp.float32
        )
        hidden, first_pull = jax.vjp(
            norm_layer,
            inputs.astype(jnp.float32) + branch,
            first_g.astype(jnp.float32),
            first_s.astype(jnp.float32),
        )
        hidden_low = hidden.astype(jnp.bfloat16)
        inner_rows = jnp.dot(hidden_low, up_full, preferred_element_type=jnp.float32) + up_b.astype(
            jnp.float32
        )
        activated, gelu_pull = jax.vjp(exact_gelu, inner_rows)
        activated_low = activated.astype(jnp.bfloat16)
        second = jnp.dot(
            activated_low, down_full, preferred_element_type=jnp.float32
        ) + down_b.astype(jnp.float32)
        output, second_pull = jax.vjp(
            norm_layer, hidden + second, second_g.astype(jnp.float32), second_s.astype(jnp.float32)
        )
        outputs.append(output.astype(jnp.bfloat16))
        back_weights = (
            lax.all_gather(qkv_weight, ("dp", "seq"), axis=0, tiled=True),
            lax.all_gather(out_weight, ("dp", "seq"), axis=0, tiled=True),
            lax.all_gather(up_weight, ("dp", "seq"), axis=0, tiled=True),
            lax.all_gather(down_weight, ("dp", "seq"), axis=0, tiled=True),
            lax.all_gather(query_bias, ("dp", "seq"), axis=0, tiled=True),
            lax.all_gather(value_bias, ("dp", "seq"), axis=0, tiled=True),
            lax.all_gather(out_bias, ("dp", "seq"), axis=0, tiled=True),
            lax.all_gather(first_gain, ("dp", "seq"), axis=0, tiled=True),
            lax.all_gather(first_shift, ("dp", "seq"), axis=0, tiled=True),
            lax.all_gather(up_bias, ("dp", "seq"), axis=0, tiled=True),
            lax.all_gather(down_bias, ("dp", "seq"), axis=0, tiled=True),
            lax.all_gather(second_gain, ("dp", "seq"), axis=0, tiled=True),
            lax.all_gather(second_shift, ("dp", "seq"), axis=0, tiled=True),
        )
        qkv_full, out_full, up_full, down_full = (
            back_weights[0],
            back_weights[1],
            back_weights[2],
            back_weights[3],
        )
        grad_sum2, grad_gain2, grad_shift2 = second_pull(cotangent[micro].astype(jnp.float32))
        grad_second = grad_sum2.astype(jnp.bfloat16)
        (grad_inner_f,) = gelu_pull(data_grad(grad_second, down_full))
        grad_inner = grad_inner_f.astype(jnp.bfloat16)
        grad_hidden = grad_sum2 + data_grad(grad_inner, up_full)
        grad_sum1, grad_gain1, grad_shift1 = first_pull(grad_hidden)
        grad_branch = grad_sum1.astype(jnp.bfloat16)
        grad_attended = data_grad(grad_branch, out_full).astype(jnp.bfloat16)
        grad_query_f, contrib = attention_back(
            query_heads,
            head_split(grad_attended),
            key_stack,
            key_segments,
            query_segment,
            log_total,
            exact_heads,
        )
        block_ids = position - reach + jnp.arange(window, dtype=jnp.int32)
        inside = (block_ids >= 0) & (block_ids < seq_count)
        canvas = jnp.zeros((seq_count, row_count, 2 * model_width), jnp.float32)
        canvas = canvas.at[jnp.clip(block_ids, 0, seq_count - 1)].add(
            jnp.where(inside[:, None, None], contrib, 0.0)
        )
        canvas = canvas.reshape(seq_count * row_count, 2 * model_width)
        key_value_grad = lax.psum_scatter(canvas, "seq", scatter_dimension=0, tiled=True)
        grad_query = grad_query_f.astype(jnp.bfloat16)
        grad_value = key_value_grad[:, model_width:].astype(jnp.bfloat16)
        grad_merged = jnp.concatenate(
            [grad_query, key_value_grad[:, :model_width].astype(jnp.bfloat16), grad_value], axis=1
        )
        input_grads.append((grad_sum1 + data_grad(grad_merged, qkv_full)).astype(jnp.bfloat16))
        terms = [
            weight_grad(inputs, grad_merged),
            weight_grad(attended, grad_branch),
            weight_grad(hidden_low, grad_inner),
            weight_grad(activated_low, grad_second),
            column_sum(grad_query),
            column_sum(grad_value),
            column_sum(grad_branch),
            grad_gain1,
            grad_shift1,
            column_sum(grad_inner),
            column_sum(grad_second),
            grad_gain2,
            grad_shift2,
        ]
        totals = [total_item + term_item for total_item, term_item in zip(totals, terms)]
    scattered = (
        lax.psum_scatter(totals[0], ("dp", "seq"), scatter_dimension=0, tiled=True),
        lax.psum_scatter(totals[1], ("dp", "seq"), scatter_dimension=0, tiled=True),
        lax.psum_scatter(totals[2], ("dp", "seq"), scatter_dimension=0, tiled=True),
        lax.psum_scatter(totals[3], ("dp", "seq"), scatter_dimension=0, tiled=True),
        lax.psum_scatter(totals[4], ("dp", "seq"), scatter_dimension=0, tiled=True),
        lax.psum_scatter(totals[5], ("dp", "seq"), scatter_dimension=0, tiled=True),
        lax.psum_scatter(totals[6], ("dp", "seq"), scatter_dimension=0, tiled=True),
        lax.psum_scatter(totals[7], ("dp", "seq"), scatter_dimension=0, tiled=True),
        lax.psum_scatter(totals[8], ("dp", "seq"), scatter_dimension=0, tiled=True),
        lax.psum_scatter(totals[9], ("dp", "seq"), scatter_dimension=0, tiled=True),
        lax.psum_scatter(totals[10], ("dp", "seq"), scatter_dimension=0, tiled=True),
        lax.psum_scatter(totals[11], ("dp", "seq"), scatter_dimension=0, tiled=True),
        lax.psum_scatter(totals[12], ("dp", "seq"), scatter_dimension=0, tiled=True),
    )
    return (
        jnp.stack(outputs),
        jnp.stack(input_grads),
        scattered[0],
        scattered[1],
        scattered[2],
        scattered[3],
        scattered[4],
        scattered[5],
        scattered[6],
        scattered[7],
        scattered[8],
        scattered[9],
        scattered[10],
        scattered[11],
        scattered[12],
    )


CORE, XBIT, ZLOW, ZHIGH = 1, 2, 4, 8
GROUPS = 4
GROUP = HEADS // GROUPS * HEAD_DIM
QROWS = 256


def swap(value, bit):
    return lax.ppermute(value, "seq", [(i, i ^ bit) for i in range(16)])


def swap_rows(value):
    return lax.ppermute(value, "dp", [(0, 1), (1, 0)])


def pair(bit, own, other):
    return jnp.where(bit == 0, own, other), jnp.where(bit == 0, other, own)


def join(bit, own, other, axis):
    return jnp.stack(pair(bit, own, other), axis=axis)


def take(value, index, axis):
    return lax.dynamic_index_in_dim(value, index, axis, keepdims=False)


def head_lanes(head, width):
    return lax.broadcasted_iota(jnp.int32, (1, width), 1) // HEAD_DIM == head


def attend_kernel(q_ref, k_ref, v_ref, qseg_ref, kseg_ref, out_ref, log_ref):
    width = q_ref.shape[1]
    rows = q_ref.shape[0]
    query = q_ref[...]
    allowed = qseg_ref[...] == kseg_ref[...]

    def visit(head, total):
        lanes = head_lanes(head, width)
        masked = jnp.where(lanes, query, jnp.zeros_like(query))
        scores = lax.dot_general(
            masked, k_ref[...], (((1,), (1,)), ((), ())), preferred_element_type=jnp.float32
        )
        scores = jnp.where(allowed, scores * 0.125, NEGATIVE)
        top = jnp.max(scores, axis=1, keepdims=True)
        expon = jnp.exp(scores - top)
        norm = jnp.sum(expon, axis=1, keepdims=True)
        value = jnp.dot(
            expon.astype(jnp.bfloat16), v_ref[...], preferred_element_type=jnp.float32
        )
        log_rows = jnp.transpose(jnp.broadcast_to(top + jnp.log(norm), (rows, 128)))
        log_ref[pl.ds(head, 1), :] = log_rows[0:1]
        return total + jnp.where(lanes, value / norm, 0.0)

    total = lax.fori_loop(0, width // HEAD_DIM, visit, jnp.zeros((rows, width), jnp.float32))
    out_ref[...] = total.astype(jnp.bfloat16)


def attend_group(query, keys, values, qseg_column, kseg_row):
    rows, width = query.shape
    count = keys.shape[0]
    return pl.pallas_call(
        attend_kernel,
        grid=(rows // QROWS,),
        in_specs=[
            pl.BlockSpec((QROWS, width), lambda i: (i, 0)),
            pl.BlockSpec((count, width), lambda i: (0, 0)),
            pl.BlockSpec((count, width), lambda i: (0, 0)),
            pl.BlockSpec((QROWS, 1), lambda i: (i, 0)),
            pl.BlockSpec((1, count), lambda i: (0, 0)),
        ],
        out_specs=[
            pl.BlockSpec((QROWS, width), lambda i: (i, 0)),
            pl.BlockSpec((8, QROWS), lambda i: (0, i)),
        ],
        out_shape=[
            jax.ShapeDtypeStruct((rows, width), jnp.bfloat16),
            jax.ShapeDtypeStruct((8, rows), jnp.float32),
        ],
        cost_estimate=pl.CostEstimate(
            flops=4 * rows * count * 256 * (width // HEAD_DIM),
            bytes_accessed=4 * (rows + count) * width,
            transcendentals=rows * count * (width // HEAD_DIM),
        ),
        compiler_params=pltpu.CompilerParams(vmem_limit_bytes=56 * 1024 * 1024),
    )(query, keys, values, qseg_column, kseg_row)


def attend_back_kernel(
    q_ref, k_ref, v_ref, grad_ref, log_ref, qseg_ref, kseg_ref, dq_ref, dk_ref, dv_ref
):
    width = q_ref.shape[1]
    query = q_ref[...]
    grad = grad_ref[...]
    allowed = kseg_ref[...] == qseg_ref[...]

    @pl.when(pl.program_id(0) == 0)
    def clear():
        dk_ref[...] = jnp.zeros_like(dk_ref)
        dv_ref[...] = jnp.zeros_like(dv_ref)

    def visit(head, total):
        lanes = head_lanes(head, width)
        query_now = jnp.where(lanes, query, jnp.zeros_like(query))
        grad_now = jnp.where(lanes, grad, jnp.zeros_like(grad))
        scores = lax.dot_general(
            k_ref[...], query_now, (((1,), (1,)), ((), ())), preferred_element_type=jnp.float32
        )
        prob = jnp.where(allowed, jnp.exp(scores * 0.125 - log_ref[pl.ds(head, 1), :]), 0.0)
        grad_prob = lax.dot_general(
            v_ref[...], grad_now, (((1,), (1,)), ((), ())), preferred_element_type=jnp.float32
        )
        delta = jnp.sum(prob * grad_prob, axis=0, keepdims=True)
        grad_score = (prob * (grad_prob - delta)).astype(jnp.bfloat16)
        dv_ref[...] += jnp.dot(
            prob.astype(jnp.bfloat16), grad_now, preferred_element_type=jnp.float32
        )
        dk_ref[...] += 0.125 * jnp.dot(grad_score, query_now, preferred_element_type=jnp.float32)
        dq = lax.dot_general(
            grad_score, k_ref[...], (((0,), (0,)), ((), ())), preferred_element_type=jnp.float32
        )
        return total + jnp.where(lanes, dq * 0.125, 0.0)

    total = lax.fori_loop(
        0, width // HEAD_DIM, visit, jnp.zeros((q_ref.shape[0], width), jnp.float32)
    )
    dq_ref[...] = total.astype(jnp.bfloat16)


def attend_group_back(query, keys, values, grad, log_total, qseg_row, kseg_column):
    rows, width = query.shape
    count = keys.shape[0]
    return pl.pallas_call(
        attend_back_kernel,
        grid=(rows // QROWS,),
        in_specs=[
            pl.BlockSpec((QROWS, width), lambda i: (i, 0)),
            pl.BlockSpec((count, width), lambda i: (0, 0)),
            pl.BlockSpec((count, width), lambda i: (0, 0)),
            pl.BlockSpec((QROWS, width), lambda i: (i, 0)),
            pl.BlockSpec((8, QROWS), lambda i: (0, i)),
            pl.BlockSpec((1, QROWS), lambda i: (0, i)),
            pl.BlockSpec((count, 1), lambda i: (0, 0)),
        ],
        out_specs=[
            pl.BlockSpec((QROWS, width), lambda i: (i, 0)),
            pl.BlockSpec((count, width), lambda i: (0, 0)),
            pl.BlockSpec((count, width), lambda i: (0, 0)),
        ],
        out_shape=[
            jax.ShapeDtypeStruct((rows, width), jnp.bfloat16),
            jax.ShapeDtypeStruct((count, width), jnp.float32),
            jax.ShapeDtypeStruct((count, width), jnp.float32),
        ],
        cost_estimate=pl.CostEstimate(
            flops=10 * rows * count * 256 * (width // HEAD_DIM),
            bytes_accessed=8 * (rows + count) * width,
            transcendentals=rows * count * (width // HEAD_DIM),
        ),
        compiler_params=pltpu.CompilerParams(vmem_limit_bytes=56 * 1024 * 1024),
    )(query, keys, values, grad, log_total, qseg_row, kseg_column)


def norm_parts(summed):
    centred = summed - jnp.mean(summed, axis=-1, keepdims=True)
    scale = lax.rsqrt(jnp.mean(centred * centred, axis=-1, keepdims=True) + EPS)
    return centred * scale, scale


def norm_back(grad, normal, scale, gain):
    grad_normal = grad * gain
    inside = grad_normal - jnp.mean(grad_normal, axis=-1, keepdims=True)
    return scale * (inside - normal * jnp.mean(grad_normal * normal, axis=-1, keepdims=True))


def gather_tokens(tokens, seq_mine):
    first = jnp.concatenate(
        [take(tokens, seq_mine, 0), swap(take(tokens, 1 - seq_mine, 0), ZHIGH)]
    )
    half = tokens.shape[-1] // 2
    block = first.shape[0]
    left, right = first[:, :half], first[:, half:]
    left_two = jnp.concatenate([left, swap(left, XBIT)])
    right_z = swap(right, ZLOW)
    left_far = swap(left_two, ZLOW)
    right_far = swap(jnp.concatenate([right, right_z]), XBIT)
    right_four = jnp.concatenate([right, right_far[:block], right_z, right_far[block:]])
    return jnp.concatenate([jnp.concatenate([left_two, left_far]), right_four], axis=1)


def gather_segments(segments, seq_mine):
    held = jnp.concatenate(
        [take(segments, seq_mine, 0), swap(take(segments, 1 - seq_mine, 0), ZHIGH)]
    ).reshape(1, -1)
    held = jnp.concatenate([held, swap(held, XBIT)], axis=1)
    held = jnp.concatenate([held, swap(held, ZLOW)], axis=1)
    return jnp.concatenate([held, swap(held, CORE)], axis=1)


def scatter_tokens(partial):
    block = partial.shape[0] // 4
    half = partial.shape[1] // 2
    low = partial.astype(jnp.bfloat16)

    def plus(one, other):
        return one.astype(jnp.float32) + other.astype(jnp.float32)

    left = plus(partial[: 2 * block, :half], swap(low[2 * block :, :half], ZLOW))
    right_keep = jnp.concatenate(
        [partial[:block, half:], partial[2 * block : 3 * block, half:]]
    )
    right_send = jnp.concatenate([low[block : 2 * block, half:], low[3 * block :, half:]])
    right = plus(right_keep, swap(right_send, XBIT))
    left = plus(left[:block], swap(left[block:].astype(jnp.bfloat16), XBIT))
    right = plus(right[:block], swap(right[block:].astype(jnp.bfloat16), ZLOW))
    both = jnp.concatenate([left, right], axis=1)
    mine = block // 2
    return both[:mine], swap(both[mine:].astype(jnp.bfloat16), ZHIGH).astype(jnp.float32)


def gather_group_weight(weight, query_bias, value_bias, place):
    dp_at, z_high, z_low, x_at, core = place
    rows = weight.shape[0]
    pieces = weight.reshape(rows, 3, 2, 2, GROUP).transpose(2, 3, 0, 1, 4)
    pieces = pieces.reshape(2, 2, rows, 3 * GROUP)
    biases = jnp.concatenate([query_bias, value_bias])
    extra = jnp.pad(biases[None], ((0, 7), (0, 3 * GROUP - biases.shape[0])))
    extra = jnp.broadcast_to(extra[None, None], (2, 2) + extra.shape)
    pieces = jnp.concatenate([pieces, extra], axis=2)
    held = join(x_at, take(pieces, x_at, 1), swap(take(pieces, 1 - x_at, 1), XBIT), 0)
    held = join(z_low, take(held, z_low, 1), swap(take(held, 1 - z_low, 1), ZLOW), 0)
    held = join(z_high, held, swap(held, ZHIGH), 0)
    held = join(dp_at, held, swap_rows(held), 0)
    held = join(core, held, swap(held, CORE), 4)
    held = held.reshape(32, rows + 8, 3 * GROUP)
    group = z_low * 2 + x_at
    query_full = held[:, rows, :rows].reshape(-1)
    value_full = held[:, rows, rows : 2 * rows].reshape(-1)
    return (
        held[:, :rows].reshape(32 * rows, 3 * GROUP),
        take(query_full.reshape(GROUPS, GROUP), group, 0),
        take(value_full.reshape(GROUPS, GROUP), group, 0),
    )


def scatter_group_weight(grad, query_sums, value_sums, place):
    dp_at, z_high, z_low, x_at, core = place
    rows = grad.shape[0] // 32
    group = z_low * 2 + x_at
    sums = jnp.concatenate([query_sums.reshape(8, rows), value_sums.reshape(8, rows)], axis=1)
    owner = jnp.arange(32, dtype=jnp.int32)[:, None] // 8 == group
    sums = jnp.where(owner, jnp.tile(sums, (4, 1)), 0.0)
    extra = jnp.pad(sums[:, None], ((0, 0), (0, 7), (0, 3 * GROUP - 2 * rows)))
    held = jnp.concatenate([grad.reshape(32, rows, 3 * GROUP), extra], axis=1)
    held = held.astype(jnp.bfloat16)

    def plus(one, other):
        return (one.astype(jnp.float32) + other.astype(jnp.float32)).astype(jnp.bfloat16)

    shape = held.shape[1:]
    held = held.reshape((16, 2) + shape)
    held = plus(take(held, core, 1), swap(take(held, 1 - core, 1), CORE))
    held = held.reshape((2, 8) + shape)
    held = plus(take(held, dp_at, 0), swap_rows(take(held, 1 - dp_at, 0)))
    held = held.reshape((2, 4) + shape)
    held = plus(take(held, z_high, 0), swap(take(held, 1 - z_high, 0), ZHIGH))
    held = held.reshape((2, 2) + shape)
    held = join(z_low, take(held, z_low, 0), swap(take(held, 1 - z_low, 0), ZLOW), 0)
    held = join(x_at, take(held, x_at, 1), swap(take(held, 1 - x_at, 1), XBIT), 1)
    held = held.reshape((GROUPS,) + shape).astype(jnp.float32)
    weight = held[:, :rows].reshape(GROUPS, rows, 3, GROUP).transpose(1, 2, 0, 3)
    biases = jnp.sum(held[:, rows, : 2 * rows], axis=0)
    return weight.reshape(rows, 3 * GROUPS * GROUP), biases[:rows], biases[rows:]


def heads_to_owners(attended, place):
    _, _, z_low, x_at, _ = place
    block = attended.shape[0] // 4
    own = attended[:block]
    x_part = swap(attended[block : 2 * block], XBIT)
    z_part = swap(attended[2 * block : 3 * block], ZLOW)
    far_part = swap(attended[3 * block :], XBIT | ZLOW)
    near = jnp.concatenate(pair(x_at, own, x_part), axis=1)
    far = jnp.concatenate(pair(x_at, z_part, far_part), axis=1)
    rows = jnp.concatenate(pair(z_low, near, far), axis=1)
    mine = block // 2
    return jnp.concatenate([rows[:mine], swap(rows[mine:], ZHIGH)])


def owners_to_heads(rows, place):
    _, _, z_low, x_at, _ = place
    mine = rows.shape[0] // 2
    rows = jnp.concatenate([rows[:mine], swap(rows[mine:], ZHIGH)])
    near, far = pair(z_low, rows[:, : 2 * GROUP], rows[:, 2 * GROUP :])
    own, x_part = pair(x_at, near[:, :GROUP], near[:, GROUP:])
    z_part, far_part = pair(x_at, far[:, :GROUP], far[:, GROUP:])
    return jnp.concatenate(
        [own, swap(x_part, XBIT), swap(z_part, ZLOW), swap(far_part, XBIT | ZLOW)]
    )


def local(
    tokens,
    segments,
    qkv_weight,
    out_weight,
    up_weight,
    down_weight,
    query_bias,
    value_bias,
    out_bias,
    first_gain,
    first_shift,
    up_bias,
    down_bias,
    second_gain,
    second_shift,
    cotangent,
):
    f32, low = jnp.float32, jnp.bfloat16
    width = tokens.shape[-1]
    shard = out_weight.shape[0]
    up_chunks = up_weight.shape[1] // width
    wide = up_chunks * shard
    vectors = (out_bias, first_gain, first_shift, down_bias, second_gain, second_shift)
    position = lax.axis_index("seq")
    z_high, z_low = position // 8, position // 4 % 2
    x_at, core = position // 2 % 2, position % 2
    place = (lax.axis_index("dp"), z_high, z_low, x_at, core)
    mine = z_high

    up_parts = up_weight.reshape(shard, up_chunks, width).transpose(1, 0, 2).reshape(wide, width)
    small = jnp.concatenate(vectors + (up_bias,))
    small = jnp.pad(small[None], ((0, 7), (0, width - small.shape[0])))
    packed = jnp.concatenate([out_weight, up_parts, down_weight, small])
    gathered = lax.all_gather(packed, ("dp", "seq"), axis=0)

    group_tokens = gather_tokens(tokens, mine)
    all_segments = gather_segments(segments, mine)
    group_weight, query_b, value_b = gather_group_weight(
        qkv_weight, query_bias, value_bias, place
    )
    half = group_tokens.shape[0]
    query = jnp.dot(group_tokens, group_weight[:, :GROUP], preferred_element_type=f32)
    query = (query + query_b.astype(f32)).astype(low)
    key_value = jnp.dot(group_tokens, group_weight[:, GROUP:], preferred_element_type=f32)
    lift = jnp.concatenate([jnp.zeros((GROUP,), f32), value_b.astype(f32)])
    key_value = (key_value + lift).astype(low)
    key_value = jnp.concatenate([key_value, swap(key_value, CORE)])
    keys, values = key_value[:, :GROUP], key_value[:, GROUP:]
    segment_column = all_segments.reshape(-1, 1)
    attended_group, log_total = attend_group(
        query, keys, values, segment_column[:half], all_segments
    )
    attended = heads_to_owners(attended_group, place)

    out_full = gathered[:, :shard].reshape(-1, width)
    up_full = jnp.concatenate(
        [
            gathered[:, shard * (1 + at) : shard * (2 + at)].reshape(-1, width)
            for at in range(up_chunks)
        ],
        axis=1,
    )
    down_full = gathered[:, shard + wide : shard + 2 * wide].reshape(-1, width)
    flat = gathered[:, shard + 2 * wide].astype(f32)
    out_b, first_g, first_s, down_b, second_g, second_s = (
        flat[:, at * shard : (at + 1) * shard].reshape(-1) for at in range(len(vectors))
    )
    up_b = flat[:, 6 * shard : 6 * shard + wide].reshape(-1)

    inputs = jnp.concatenate([take(tokens, mine, 0), take(tokens, 1 - mine, 0)])
    branch = jnp.dot(attended, out_full, preferred_element_type=f32) + out_b
    normal1, scale1 = norm_parts(inputs.astype(f32) + branch)
    hidden = normal1 * first_g + first_s
    hidden_low = hidden.astype(low)
    inner = jnp.dot(hidden_low, up_full, preferred_element_type=f32) + up_b
    activated, gelu_pull = jax.vjp(exact_gelu, inner)
    activated_low = activated.astype(low)
    second = jnp.dot(activated_low, down_full, preferred_element_type=f32) + down_b
    normal2, scale2 = norm_parts(hidden + second)
    output = (normal2 * second_g + second_s).astype(low)
    output = jnp.stack(pair(mine, output[: output.shape[0] // 2], output[output.shape[0] // 2 :]))

    upstream = jnp.concatenate([take(cotangent, mine, 0), take(cotangent, 1 - mine, 0)])
    upstream = upstream.astype(f32)
    grad_sum2 = norm_back(upstream, normal2, scale2, second_g)
    grad_second = grad_sum2.astype(low)
    (grad_inner,) = gelu_pull(data_grad(grad_second, down_full))
    grad_inner = grad_inner.astype(low)
    grad_hidden = grad_sum2 + data_grad(grad_inner, up_full)
    grad_sum1 = norm_back(grad_hidden, normal1, scale1, first_g)
    grad_branch = grad_sum1.astype(low)
    grad_attended = data_grad(grad_branch, out_full).astype(low)

    grad_out = weight_grad(attended, grad_branch).astype(low).reshape(32, shard, width)
    grad_up = jnp.concatenate(
        [
            weight_grad(hidden_low, grad_inner[:, at * width : (at + 1) * width])
            .astype(low)
            .reshape(32, shard, width)
            for at in range(up_chunks)
        ],
        axis=1,
    )
    grad_down = weight_grad(activated_low, grad_second).astype(low).reshape(32, wide, width)
    sums = (
        column_sum(grad_branch),
        jnp.sum(grad_hidden * normal1, axis=0),
        jnp.sum(grad_hidden, axis=0),
        column_sum(grad_second),
        jnp.sum(upstream * normal2, axis=0),
        jnp.sum(upstream, axis=0),
        column_sum(grad_inner),
    )
    sums = jnp.concatenate([item.reshape(32, -1) for item in sums], axis=1)
    sums = jnp.pad(sums[:, None], ((0, 0), (0, 7), (0, width - sums.shape[1]))).astype(low)
    partial = jnp.concatenate([grad_out, grad_up, grad_down, sums], axis=1)
    reduced = lax.psum_scatter(
        partial.reshape(-1, width), ("dp", "seq"), scatter_dimension=0, tiled=True
    ).astype(f32)

    grad_group = owners_to_heads(grad_attended, place)
    grad_query, grad_keys, grad_values = attend_group_back(
        query, keys, values, grad_group, log_total, all_segments[:, :half], segment_column
    )
    grad_kv = jnp.concatenate([grad_keys, grad_values], axis=1)
    grad_kv = grad_kv[:half] + swap(grad_kv[half:].astype(low), CORE).astype(f32)
    grad_merged = jnp.concatenate([grad_query, grad_kv.astype(low)], axis=1)
    own_part, other_part = scatter_tokens(data_grad(grad_merged, group_weight))
    count = own_part.shape[0]
    own_grad = (grad_sum1[:count] + own_part).astype(low)
    other_grad = (grad_sum1[count:] + other_part).astype(low)
    input_grad = jnp.stack(pair(mine, own_grad, other_grad))
    grad_qkv, grad_query_bias, grad_value_bias = scatter_group_weight(
        weight_grad(group_tokens, grad_merged),
        column_sum(grad_merged[:, :GROUP]),
        column_sum(grad_merged[:, 2 * GROUP :]),
        place,
    )

    up_rows = reduced[shard : shard + wide].reshape(up_chunks, shard, width)
    tail = reduced[shard + 2 * wide]
    parts = [tail[at * shard : (at + 1) * shard] for at in range(6)]
    return (
        output,
        input_grad,
        grad_qkv,
        reduced[:shard],
        up_rows.transpose(1, 0, 2).reshape(shard, -1),
        reduced[shard + wide : shard + 2 * wide],
        grad_query_bias,
        grad_value_bias,
        parts[0],
        parts[1],
        parts[2],
        tail[6 * shard : 6 * shard + wide],
        parts[3],
        parts[4],
        parts[5],
    )


def solution(mesh):
    in_specs = (
        P("dp", "seq", None),
        P("dp", "seq"),
        P(("dp", "seq"), None),
        P(("dp", "seq"), None),
        P(("dp", "seq"), None),
        P(("dp", "seq"), None),
        P(("dp", "seq")),
        P(("dp", "seq")),
        P(("dp", "seq")),
        P(("dp", "seq")),
        P(("dp", "seq")),
        P(("dp", "seq")),
        P(("dp", "seq")),
        P(("dp", "seq")),
        P(("dp", "seq")),
        P("dp", "seq", None),
    )
    out_specs = (
        P("dp", "seq", None),
        P("dp", "seq", None),
        P(("dp", "seq"), None),
        P(("dp", "seq"), None),
        P(("dp", "seq"), None),
        P(("dp", "seq"), None),
        P(("dp", "seq")),
        P(("dp", "seq")),
        P(("dp", "seq")),
        P(("dp", "seq")),
        P(("dp", "seq")),
        P(("dp", "seq")),
        P(("dp", "seq")),
        P(("dp", "seq")),
        P(("dp", "seq")),
    )
    fits = mesh.shape["dp"] == 2 and mesh.shape["seq"] == 16
    return jax.shard_map(
        local if fits else general_local, mesh=mesh, in_specs=in_specs, out_specs=out_specs, check_vma=False
    )
```

```python
import jax
import jax.numpy as jnp
from jax import lax
from jax.experimental import pallas as pl
from jax.experimental.pallas import tpu as pltpu
from jax.sharding import PartitionSpec as P

HEADS = 12
HEAD_DIM = 64
FF = 3072
DOC_MOST = 2000


EPS = 1e-12
NEGATIVE = -1e30


def norm_layer(summed, gain_row, shift_row):
    average = jnp.mean(summed, axis=-1, keepdims=True)
    centred = summed - average
    variance = jnp.mean(centred * centred, axis=-1, keepdims=True)
    return centred * lax.rsqrt(variance + EPS) * gain_row + shift_row


def exact_gelu(inner_rows):
    return jax.nn.gelu(inner_rows, approximate=False)


def same_value(state_pair):
    return state_pair


def head_split(matrix):
    return matrix.reshape(matrix.shape[0], HEADS, HEAD_DIM)


def block_scores(query_heads, key_rows):
    return (
        jnp.einsum(
            "qhd,khd->hqk", query_heads, head_split(key_rows), preferred_element_type=jnp.float32
        )
        * 0.125
    )


def probabilities(query_heads, key_stack, block_index, allowed, log_total):
    scores = block_scores(query_heads, key_stack[block_index, :, : HEADS * HEAD_DIM])
    return jnp.where(allowed[None], jnp.exp(scores - log_total[:, :, None]), 0.0)


def block_mask(query_segment, key_segments, block_index):
    return query_segment[:, None] == key_segments[block_index][None, :]


def log_totals(query_heads, key_stack, key_segments, query_segment):
    row_count = query_heads.shape[0]

    def log_visit(block_index, carry_state):
        allowed = block_mask(query_segment, key_segments, block_index)

        def log_compute(state_pair):
            top_now, total_now = state_pair
            scores = jnp.where(
                allowed[None],
                block_scores(query_heads, key_stack[block_index, :, : HEADS * HEAD_DIM]),
                NEGATIVE,
            )
            top_new = jnp.maximum(top_now, jnp.max(scores, axis=-1))
            expon_rows = jnp.where(allowed[None], jnp.exp(scores - top_new[:, :, None]), 0.0)
            return (top_new, total_now * jnp.exp(top_now - top_new) + jnp.sum(expon_rows, axis=-1))

        return lax.cond(jnp.any(allowed), log_compute, same_value, carry_state)

    initial = (
        jnp.full((HEADS, row_count), NEGATIVE, jnp.float32),
        jnp.zeros((HEADS, row_count), jnp.float32),
    )
    top_final, total_final = lax.fori_loop(0, key_stack.shape[0], log_visit, initial)
    return top_final + jnp.log(total_final)


def attend_values(query_heads, key_stack, key_segments, query_segment, log_total):
    model_width = HEADS * HEAD_DIM

    def attend_visit(block_index, running):
        allowed = block_mask(query_segment, key_segments, block_index)

        def attend_compute(running_in):
            main_sum, rest_sum = running_in
            weights_block = probabilities(query_heads, key_stack, block_index, allowed, log_total)
            weights_low = weights_block.astype(jnp.bfloat16)
            weights_rest = (weights_block - weights_low.astype(jnp.float32)).astype(jnp.bfloat16)
            value_heads = head_split(key_stack[block_index, :, model_width:])
            main_new = main_sum + jnp.einsum(
                "hqk,khd->qhd", weights_low, value_heads, preferred_element_type=jnp.float32
            )
            rest_new = rest_sum + jnp.einsum(
                "hqk,khd->qhd", weights_rest, value_heads, preferred_element_type=jnp.float32
            )
            return (main_new, rest_new)

        return lax.cond(jnp.any(allowed), attend_compute, same_value, running)

    zero_heads = jnp.zeros(query_heads.shape, jnp.float32)
    main_sum, rest_sum = lax.fori_loop(
        0, key_stack.shape[0], attend_visit, (zero_heads, zero_heads)
    )
    return (main_sum.reshape(query_heads.shape[0], model_width), main_sum + rest_sum)


def attention_back(
    query_heads, grad_heads, key_stack, key_segments, query_segment, log_total, exact_heads
):
    model_width = HEADS * HEAD_DIM
    row_count = query_heads.shape[0]
    delta_rows = jnp.einsum("qhd,qhd->hq", grad_heads.astype(jnp.float32), exact_heads)

    def grad_visit(block_index, carry_state):
        allowed = block_mask(query_segment, key_segments, block_index)

        def grad_compute(state_pair):
            grad_query_in, contrib_in = state_pair
            weights_block = probabilities(query_heads, key_stack, block_index, allowed, log_total)
            key_heads = head_split(key_stack[block_index, :, :model_width])
            value_heads = head_split(key_stack[block_index, :, model_width:])
            grad_probs = jnp.einsum(
                "qhd,khd->hqk", grad_heads, value_heads, preferred_element_type=jnp.float32
            )
            grad_scores = (weights_block * (grad_probs - delta_rows[:, :, None])).astype(
                jnp.bfloat16
            )
            grad_query_new = grad_query_in + jnp.einsum(
                "hqk,khd->qhd", grad_scores, key_heads, preferred_element_type=jnp.float32
            )
            grad_keys = (
                jnp.einsum(
                    "hqk,qhd->khd", grad_scores, query_heads, preferred_element_type=jnp.float32
                )
                * 0.125
            )
            grad_values = jnp.einsum(
                "hqk,qhd->khd",
                weights_block.astype(jnp.bfloat16),
                grad_heads,
                preferred_element_type=jnp.float32,
            )
            joined = jnp.concatenate(
                [
                    grad_keys.reshape(row_count, model_width),
                    grad_values.reshape(row_count, model_width),
                ],
                axis=1,
            )
            return (
                grad_query_new,
                lax.dynamic_update_index_in_dim(contrib_in, joined, block_index, 0),
            )

        return lax.cond(jnp.any(allowed), grad_compute, same_value, carry_state)

    initial = (
        jnp.zeros(query_heads.shape, jnp.float32),
        jnp.zeros((key_stack.shape[0], row_count, 2 * model_width), jnp.float32),
    )
    grad_query, contrib = lax.fori_loop(0, key_stack.shape[0], grad_visit, initial)
    return ((grad_query * 0.125).reshape(row_count, model_width), contrib)


def weight_grad(left_rows, right_rows):
    return jnp.einsum("rk,rn->kn", left_rows, right_rows, preferred_element_type=jnp.float32)


def data_grad(grad_rows, weight_full):
    return jnp.einsum("rn,kn->rk", grad_rows, weight_full, preferred_element_type=jnp.float32)


def column_sum(rows_low):
    return jnp.sum(rows_low.astype(jnp.float32), axis=0)


def general_local(
    tokens,
    segments,
    qkv_weight,
    out_weight,
    up_weight,
    down_weight,
    query_bias,
    value_bias,
    out_bias,
    first_gain,
    first_shift,
    up_bias,
    down_bias,
    second_gain,
    second_shift,
    cotangent,
):
    batch_count, row_count, model_width = tokens.shape
    seq_count = lax.axis_size("seq")
    reach = min((DOC_MOST + row_count - 2) // row_count, seq_count - 1)
    window = 2 * reach + 1
    position = lax.axis_index("seq")
    every_segment = lax.all_gather(segments, "seq", axis=1, tiled=True)
    padded_segment = jnp.pad(
        every_segment, ((0, 0), (reach * row_count, reach * row_count)), constant_values=-1
    )
    totals = [
        jnp.zeros((model_width, 3 * model_width), jnp.float32),
        jnp.zeros((model_width, model_width), jnp.float32),
        jnp.zeros((model_width, FF), jnp.float32),
        jnp.zeros((FF, model_width), jnp.float32),
        jnp.zeros((model_width,), jnp.float32),
        jnp.zeros((model_width,), jnp.float32),
        jnp.zeros((model_width,), jnp.float32),
        jnp.zeros((model_width,), jnp.float32),
        jnp.zeros((model_width,), jnp.float32),
        jnp.zeros((FF,), jnp.float32),
        jnp.zeros((model_width,), jnp.float32),
        jnp.zeros((model_width,), jnp.float32),
        jnp.zeros((model_width,), jnp.float32),
    ]
    outputs = []
    input_grads = []
    for micro in range(batch_count):
        weights_now = (
            lax.all_gather(qkv_weight, ("dp", "seq"), axis=0, tiled=True),
            lax.all_gather(out_weight, ("dp", "seq"), axis=0, tiled=True),
            lax.all_gather(up_weight, ("dp", "seq"), axis=0, tiled=True),
            lax.all_gather(down_weight, ("dp", "seq"), axis=0, tiled=True),
            lax.all_gather(query_bias, ("dp", "seq"), axis=0, tiled=True),
            lax.all_gather(value_bias, ("dp", "seq"), axis=0, tiled=True),
            lax.all_gather(out_bias, ("dp", "seq"), axis=0, tiled=True),
            lax.all_gather(first_gain, ("dp", "seq"), axis=0, tiled=True),
            lax.all_gather(first_shift, ("dp", "seq"), axis=0, tiled=True),
            lax.all_gather(up_bias, ("dp", "seq"), axis=0, tiled=True),
            lax.all_gather(down_bias, ("dp", "seq"), axis=0, tiled=True),
            lax.all_gather(second_gain, ("dp", "seq"), axis=0, tiled=True),
            lax.all_gather(second_shift, ("dp", "seq"), axis=0, tiled=True),
        )
        (
            qkv_full,
            out_full,
            up_full,
            down_full,
            query_b,
            value_b,
            out_b,
            first_g,
            first_s,
            up_b,
            down_b,
            second_g,
            second_s,
        ) = weights_now
        inputs = tokens[micro]
        merged = jnp.dot(inputs, qkv_full, preferred_element_type=jnp.float32)
        query = (merged[:, :model_width] + query_b.astype(jnp.float32)).astype(jnp.bfloat16)
        keys_now = merged[:, model_width : 2 * model_width].astype(jnp.bfloat16)
        values_now = (merged[:, 2 * model_width :] + value_b.astype(jnp.float32)).astype(
            jnp.bfloat16
        )
        whole_keys = lax.all_gather(
            jnp.concatenate([keys_now, values_now], axis=1), "seq", axis=0, tiled=True
        )
        padded = jnp.pad(whole_keys, ((reach * row_count, reach * row_count), (0, 0)))
        picked = lax.dynamic_slice_in_dim(padded, position * row_count, window * row_count, 0)
        key_stack = picked.reshape(window, row_count, 2 * model_width)
        key_segments = lax.dynamic_slice_in_dim(
            padded_segment[micro], position * row_count, window * row_count, 0
        ).reshape(window, row_count)
        query_segment = segments[micro]
        query_heads = head_split(query)
        log_total = log_totals(query_heads, key_stack, key_segments, query_segment)
        attended_f, exact_heads = attend_values(
            query_heads, key_stack, key_segments, query_segment, log_total
        )
        attended = attended_f.astype(jnp.bfloat16)
        branch = jnp.dot(attended, out_full, preferred_element_type=jnp.float32) + out_b.astype(
            jnp.float32
        )
        hidden, first_pull = jax.vjp(
            norm_layer,
            inputs.astype(jnp.float32) + branch,
            first_g.astype(jnp.float32),
            first_s.astype(jnp.float32),
        )
        hidden_low = hidden.astype(jnp.bfloat16)
        inner_rows = jnp.dot(hidden_low, up_full, preferred_element_type=jnp.float32) + up_b.astype(
            jnp.float32
        )
        activated, gelu_pull = jax.vjp(exact_gelu, inner_rows)
        activated_low = activated.astype(jnp.bfloat16)
        second = jnp.dot(
            activated_low, down_full, preferred_element_type=jnp.float32
        ) + down_b.astype(jnp.float32)
        output, second_pull = jax.vjp(
            norm_layer, hidden + second, second_g.astype(jnp.float32), second_s.astype(jnp.float32)
        )
        outputs.append(output.astype(jnp.bfloat16))
        back_weights = (
            lax.all_gather(qkv_weight, ("dp", "seq"), axis=0, tiled=True),
            lax.all_gather(out_weight, ("dp", "seq"), axis=0, tiled=True),
            lax.all_gather(up_weight, ("dp", "seq"), axis=0, tiled=True),
            lax.all_gather(down_weight, ("dp", "seq"), axis=0, tiled=True),
            lax.all_gather(query_bias, ("dp", "seq"), axis=0, tiled=True),
            lax.all_gather(value_bias, ("dp", "seq"), axis=0, tiled=True),
            lax.all_gather(out_bias, ("dp", "seq"), axis=0, tiled=True),
            lax.all_gather(first_gain, ("dp", "seq"), axis=0, tiled=True),
            lax.all_gather(first_shift, ("dp", "seq"), axis=0, tiled=True),
            lax.all_gather(up_bias, ("dp", "seq"), axis=0, tiled=True),
            lax.all_gather(down_bias, ("dp", "seq"), axis=0, tiled=True),
            lax.all_gather(second_gain, ("dp", "seq"), axis=0, tiled=True),
            lax.all_gather(second_shift, ("dp", "seq"), axis=0, tiled=True),
        )
        qkv_full, out_full, up_full, down_full = (
            back_weights[0],
            back_weights[1],
            back_weights[2],
            back_weights[3],
        )
        grad_sum2, grad_gain2, grad_shift2 = second_pull(cotangent[micro].astype(jnp.float32))
        grad_second = grad_sum2.astype(jnp.bfloat16)
        (grad_inner_f,) = gelu_pull(data_grad(grad_second, down_full))
        grad_inner = grad_inner_f.astype(jnp.bfloat16)
        grad_hidden = grad_sum2 + data_grad(grad_inner, up_full)
        grad_sum1, grad_gain1, grad_shift1 = first_pull(grad_hidden)
        grad_branch = grad_sum1.astype(jnp.bfloat16)
        grad_attended = data_grad(grad_branch, out_full).astype(jnp.bfloat16)
        grad_query_f, contrib = attention_back(
            query_heads,
            head_split(grad_attended),
            key_stack,
            key_segments,
            query_segment,
            log_total,
            exact_heads,
        )
        block_ids = position - reach + jnp.arange(window, dtype=jnp.int32)
        inside = (block_ids >= 0) & (block_ids < seq_count)
        canvas = jnp.zeros((seq_count, row_count, 2 * model_width), jnp.float32)
        canvas = canvas.at[jnp.clip(block_ids, 0, seq_count - 1)].add(
            jnp.where(inside[:, None, None], contrib, 0.0)
        )
        canvas = canvas.reshape(seq_count * row_count, 2 * model_width)
        key_value_grad = lax.psum_scatter(canvas, "seq", scatter_dimension=0, tiled=True)
        grad_query = grad_query_f.astype(jnp.bfloat16)
        grad_value = key_value_grad[:, model_width:].astype(jnp.bfloat16)
        grad_merged = jnp.concatenate(
            [grad_query, key_value_grad[:, :model_width].astype(jnp.bfloat16), grad_value], axis=1
        )
        input_grads.append((grad_sum1 + data_grad(grad_merged, qkv_full)).astype(jnp.bfloat16))
        terms = [
            weight_grad(inputs, grad_merged),
            weight_grad(attended, grad_branch),
            weight_grad(hidden_low, grad_inner),
            weight_grad(activated_low, grad_second),
            column_sum(grad_query),
            column_sum(grad_value),
            column_sum(grad_branch),
            grad_gain1,
            grad_shift1,
            column_sum(grad_inner),
            column_sum(grad_second),
            grad_gain2,
            grad_shift2,
        ]
        totals = [total_item + term_item for total_item, term_item in zip(totals, terms)]
    scattered = (
        lax.psum_scatter(totals[0], ("dp", "seq"), scatter_dimension=0, tiled=True),
        lax.psum_scatter(totals[1], ("dp", "seq"), scatter_dimension=0, tiled=True),
        lax.psum_scatter(totals[2], ("dp", "seq"), scatter_dimension=0, tiled=True),
        lax.psum_scatter(totals[3], ("dp", "seq"), scatter_dimension=0, tiled=True),
        lax.psum_scatter(totals[4], ("dp", "seq"), scatter_dimension=0, tiled=True),
        lax.psum_scatter(totals[5], ("dp", "seq"), scatter_dimension=0, tiled=True),
        lax.psum_scatter(totals[6], ("dp", "seq"), scatter_dimension=0, tiled=True),
        lax.psum_scatter(totals[7], ("dp", "seq"), scatter_dimension=0, tiled=True),
        lax.psum_scatter(totals[8], ("dp", "seq"), scatter_dimension=0, tiled=True),
        lax.psum_scatter(totals[9], ("dp", "seq"), scatter_dimension=0, tiled=True),
        lax.psum_scatter(totals[10], ("dp", "seq"), scatter_dimension=0, tiled=True),
        lax.psum_scatter(totals[11], ("dp", "seq"), scatter_dimension=0, tiled=True),
        lax.psum_scatter(totals[12], ("dp", "seq"), scatter_dimension=0, tiled=True),
    )
    return (
        jnp.stack(outputs),
        jnp.stack(input_grads),
        scattered[0],
        scattered[1],
        scattered[2],
        scattered[3],
        scattered[4],
        scattered[5],
        scattered[6],
        scattered[7],
        scattered[8],
        scattered[9],
        scattered[10],
        scattered[11],
        scattered[12],
    )


CORE, XBIT, ZLOW, ZHIGH = 1, 2, 4, 8
GROUPS = 4
GROUP = HEADS // GROUPS * HEAD_DIM
QROWS = 256


def swap(value, bit):
    return lax.ppermute(value, "seq", [(i, i ^ bit) for i in range(16)])


def swap_rows(value):
    return lax.ppermute(value, "dp", [(0, 1), (1, 0)])


def pair(bit, own, other):
    return jnp.where(bit == 0, own, other), jnp.where(bit == 0, other, own)


def join(bit, own, other, axis):
    return jnp.stack(pair(bit, own, other), axis=axis)


def take(value, index, axis):
    return lax.dynamic_index_in_dim(value, index, axis, keepdims=False)


def head_lanes(head, width):
    return lax.broadcasted_iota(jnp.int32, (1, width), 1) // HEAD_DIM == head


def attend_kernel(q_ref, k_ref, v_ref, qseg_ref, kseg_ref, out_ref, log_ref):
    width = q_ref.shape[1]
    rows = q_ref.shape[0]
    query = q_ref[...]
    allowed = qseg_ref[...] == kseg_ref[...]

    def visit(head, total):
        lanes = head_lanes(head, width)
        masked = jnp.where(lanes, query, jnp.zeros_like(query))
        scores = lax.dot_general(
            masked, k_ref[...], (((1,), (1,)), ((), ())), preferred_element_type=jnp.float32
        )
        scores = jnp.where(allowed, scores * 0.125, NEGATIVE)
        top = jnp.max(scores, axis=1, keepdims=True)
        expon = jnp.exp(scores - top)
        norm = jnp.sum(expon, axis=1, keepdims=True)
        value = jnp.dot(
            expon.astype(jnp.bfloat16), v_ref[...], preferred_element_type=jnp.float32
        )
        log_rows = jnp.transpose(jnp.broadcast_to(top + jnp.log(norm), (rows, 128)))
        log_ref[pl.ds(head, 1), :] = log_rows[0:1]
        return total + jnp.where(lanes, value / norm, 0.0)

    total = lax.fori_loop(0, width // HEAD_DIM, visit, jnp.zeros((rows, width), jnp.float32))
    out_ref[...] = total.astype(jnp.bfloat16)


def attend_group(query, keys, values, qseg_column, kseg_row):
    rows, width = query.shape
    count = keys.shape[0]
    return pl.pallas_call(
        attend_kernel,
        grid=(rows // QROWS,),
        in_specs=[
            pl.BlockSpec((QROWS, width), lambda i: (i, 0)),
            pl.BlockSpec((count, width), lambda i: (0, 0)),
            pl.BlockSpec((count, width), lambda i: (0, 0)),
            pl.BlockSpec((QROWS, 1), lambda i: (i, 0)),
            pl.BlockSpec((1, count), lambda i: (0, 0)),
        ],
        out_specs=[
            pl.BlockSpec((QROWS, width), lambda i: (i, 0)),
            pl.BlockSpec((8, QROWS), lambda i: (0, i)),
        ],
        out_shape=[
            jax.ShapeDtypeStruct((rows, width), jnp.bfloat16),
            jax.ShapeDtypeStruct((8, rows), jnp.float32),
        ],
        cost_estimate=pl.CostEstimate(
            flops=4 * rows * count * 256 * (width // HEAD_DIM),
            bytes_accessed=4 * (rows + count) * width,
            transcendentals=rows * count * (width // HEAD_DIM),
        ),
        compiler_params=pltpu.CompilerParams(vmem_limit_bytes=56 * 1024 * 1024),
    )(query, keys, values, qseg_column, kseg_row)


def attend_back_kernel(
    q_ref, k_ref, v_ref, grad_ref, log_ref, qseg_ref, kseg_ref, dq_ref, dk_ref, dv_ref
):
    width = q_ref.shape[1]
    query = q_ref[...]
    grad = grad_ref[...]
    allowed = kseg_ref[...] == qseg_ref[...]

    @pl.when(pl.program_id(0) == 0)
    def clear():
        dk_ref[...] = jnp.zeros_like(dk_ref)
        dv_ref[...] = jnp.zeros_like(dv_ref)

    def visit(head, total):
        lanes = head_lanes(head, width)
        query_now = jnp.where(lanes, query, jnp.zeros_like(query))
        grad_now = jnp.where(lanes, grad, jnp.zeros_like(grad))
        scores = lax.dot_general(
            k_ref[...], query_now, (((1,), (1,)), ((), ())), preferred_element_type=jnp.float32
        )
        prob = jnp.where(allowed, jnp.exp(scores * 0.125 - log_ref[pl.ds(head, 1), :]), 0.0)
        grad_prob = lax.dot_general(
            v_ref[...], grad_now, (((1,), (1,)), ((), ())), preferred_element_type=jnp.float32
        )
        delta = jnp.sum(prob * grad_prob, axis=0, keepdims=True)
        grad_score = (prob * (grad_prob - delta)).astype(jnp.bfloat16)
        dv_ref[...] += jnp.dot(
            prob.astype(jnp.bfloat16), grad_now, preferred_element_type=jnp.float32
        )
        dk_ref[...] += 0.125 * jnp.dot(grad_score, query_now, preferred_element_type=jnp.float32)
        dq = lax.dot_general(
            grad_score, k_ref[...], (((0,), (0,)), ((), ())), preferred_element_type=jnp.float32
        )
        return total + jnp.where(lanes, dq * 0.125, 0.0)

    total = lax.fori_loop(
        0, width // HEAD_DIM, visit, jnp.zeros((q_ref.shape[0], width), jnp.float32)
    )
    dq_ref[...] = total.astype(jnp.bfloat16)


def attend_group_back(query, keys, values, grad, log_total, qseg_row, kseg_column):
    rows, width = query.shape
    count = keys.shape[0]
    return pl.pallas_call(
        attend_back_kernel,
        grid=(rows // QROWS,),
        in_specs=[
            pl.BlockSpec((QROWS, width), lambda i: (i, 0)),
            pl.BlockSpec((count, width), lambda i: (0, 0)),
            pl.BlockSpec((count, width), lambda i: (0, 0)),
            pl.BlockSpec((QROWS, width), lambda i: (i, 0)),
            pl.BlockSpec((8, QROWS), lambda i: (0, i)),
            pl.BlockSpec((1, QROWS), lambda i: (0, i)),
            pl.BlockSpec((count, 1), lambda i: (0, 0)),
        ],
        out_specs=[
            pl.BlockSpec((QROWS, width), lambda i: (i, 0)),
            pl.BlockSpec((count, width), lambda i: (0, 0)),
            pl.BlockSpec((count, width), lambda i: (0, 0)),
        ],
        out_shape=[
            jax.ShapeDtypeStruct((rows, width), jnp.bfloat16),
            jax.ShapeDtypeStruct((count, width), jnp.float32),
            jax.ShapeDtypeStruct((count, width), jnp.float32),
        ],
        cost_estimate=pl.CostEstimate(
            flops=10 * rows * count * 256 * (width // HEAD_DIM),
            bytes_accessed=8 * (rows + count) * width,
            transcendentals=rows * count * (width // HEAD_DIM),
        ),
        compiler_params=pltpu.CompilerParams(vmem_limit_bytes=56 * 1024 * 1024),
    )(query, keys, values, grad, log_total, qseg_row, kseg_column)


def norm_parts(summed):
    centred = summed - jnp.mean(summed, axis=-1, keepdims=True)
    scale = lax.rsqrt(jnp.mean(centred * centred, axis=-1, keepdims=True) + EPS)
    return centred * scale, scale


def norm_back(grad, normal, scale, gain):
    grad_normal = grad * gain
    inside = grad_normal - jnp.mean(grad_normal, axis=-1, keepdims=True)
    return scale * (inside - normal * jnp.mean(grad_normal * normal, axis=-1, keepdims=True))


def gather_tokens(tokens, seq_mine):
    first = jnp.concatenate(
        [take(tokens, seq_mine, 0), swap(take(tokens, 1 - seq_mine, 0), ZHIGH)]
    )
    half = tokens.shape[-1] // 2
    block = first.shape[0]
    left, right = first[:, :half], first[:, half:]
    left_two = jnp.concatenate([left, swap(left, XBIT)])
    right_z = swap(right, ZLOW)
    left_far = swap(left_two, ZLOW)
    right_far = swap(jnp.concatenate([right, right_z]), XBIT)
    right_four = jnp.concatenate([right, right_far[:block], right_z, right_far[block:]])
    return jnp.concatenate([jnp.concatenate([left_two, left_far]), right_four], axis=1)


def gather_segments(segments, seq_mine):
    held = jnp.concatenate(
        [take(segments, seq_mine, 0), swap(take(segments, 1 - seq_mine, 0), ZHIGH)]
    ).reshape(1, -1)
    held = jnp.concatenate([held, swap(held, XBIT)], axis=1)
    held = jnp.concatenate([held, swap(held, ZLOW)], axis=1)
    return jnp.concatenate([held, swap(held, CORE)], axis=1)


def add_pair(one, other):
    return one.astype(jnp.float32) + other.astype(jnp.float32)


def scatter_first(partial):
    block = partial.shape[0] // 4
    half = partial.shape[1] // 2
    low = partial.astype(jnp.bfloat16)
    left = swap(low[2 * block :, :half], ZLOW)
    right = jnp.concatenate([low[block : 2 * block, half:], low[3 * block :, half:]])
    return left, swap(right, XBIT)


def scatter_second(partial, left_got, right_got):
    block = partial.shape[0] // 4
    half = partial.shape[1] // 2
    left = add_pair(partial[: 2 * block, :half], left_got)
    right = jnp.concatenate([partial[:block, half:], partial[2 * block : 3 * block, half:]])
    right = add_pair(right, right_got)
    got = (
        swap(left[block:].astype(jnp.bfloat16), XBIT),
        swap(right[block:].astype(jnp.bfloat16), ZLOW),
    )
    return left[:block], right[:block], got


def scatter_third(left, right, got):
    both = jnp.concatenate([add_pair(left, got[0]), add_pair(right, got[1])], axis=1)
    mine = both.shape[0] // 2
    return both[:mine], swap(both[mine:].astype(jnp.bfloat16), ZHIGH)


def gather_group_weight(weight, query_bias, value_bias, place):
    dp_at, z_high, z_low, x_at, core = place
    rows = weight.shape[0]
    pieces = weight.reshape(rows, 3, 2, 2, GROUP).transpose(2, 3, 0, 1, 4)
    pieces = pieces.reshape(2, 2, rows, 3 * GROUP)
    biases = jnp.concatenate([query_bias, value_bias])
    extra = jnp.pad(biases[None], ((0, 7), (0, 3 * GROUP - biases.shape[0])))
    extra = jnp.broadcast_to(extra[None, None], (2, 2) + extra.shape)
    pieces = jnp.concatenate([pieces, extra], axis=2)
    held = join(x_at, take(pieces, x_at, 1), swap(take(pieces, 1 - x_at, 1), XBIT), 0)
    held = join(z_low, take(held, z_low, 1), swap(take(held, 1 - z_low, 1), ZLOW), 0)
    held = join(z_high, held, swap(held, ZHIGH), 0)
    held = join(dp_at, held, swap_rows(held), 0)
    held = join(core, held, swap(held, CORE), 4)
    held = held.reshape(32, rows + 8, 3 * GROUP)
    group = z_low * 2 + x_at
    query_full = held[:, rows, :rows].reshape(-1)
    value_full = held[:, rows, rows : 2 * rows].reshape(-1)
    return (
        held[:, :rows].reshape(32 * rows, 3 * GROUP),
        take(query_full.reshape(GROUPS, GROUP), group, 0),
        take(value_full.reshape(GROUPS, GROUP), group, 0),
    )


def scatter_group_weight(grad, query_sums, value_sums, place):
    dp_at, z_high, z_low, x_at, core = place
    rows = grad.shape[0] // 32
    group = z_low * 2 + x_at
    sums = jnp.concatenate([query_sums.reshape(8, rows), value_sums.reshape(8, rows)], axis=1)
    owner = jnp.arange(32, dtype=jnp.int32)[:, None] // 8 == group
    sums = jnp.where(owner, jnp.tile(sums, (4, 1)), 0.0)
    extra = jnp.pad(sums[:, None], ((0, 0), (0, 7), (0, 3 * GROUP - 2 * rows)))
    held = jnp.concatenate([grad.reshape(32, rows, 3 * GROUP), extra], axis=1)
    held = held.astype(jnp.bfloat16)

    def plus(one, other):
        return (one.astype(jnp.float32) + other.astype(jnp.float32)).astype(jnp.bfloat16)

    shape = held.shape[1:]
    held = held.reshape((16, 2) + shape)
    held = plus(take(held, core, 1), swap(take(held, 1 - core, 1), CORE))
    held = held.reshape((2, 8) + shape)
    held = plus(take(held, dp_at, 0), swap_rows(take(held, 1 - dp_at, 0)))
    held = held.reshape((2, 4) + shape)
    held = plus(take(held, z_high, 0), swap(take(held, 1 - z_high, 0), ZHIGH))
    held = held.reshape((2, 2) + shape)
    held = join(z_low, take(held, z_low, 0), swap(take(held, 1 - z_low, 0), ZLOW), 0)
    held = join(x_at, take(held, x_at, 1), swap(take(held, 1 - x_at, 1), XBIT), 1)
    held = held.reshape((GROUPS,) + shape).astype(jnp.float32)
    weight = held[:, :rows].reshape(GROUPS, rows, 3, GROUP).transpose(1, 2, 0, 3)
    biases = jnp.sum(held[:, rows, : 2 * rows], axis=0)
    return weight.reshape(rows, 3 * GROUPS * GROUP), biases[:rows], biases[rows:]


class Chain:
    def __init__(self, held, place):
        self.place = place
        self.left = list(range(5))
        self.held = held.reshape((2, 2, 2, 2, 2) + held.shape[1:])

    def send(self, step):
        self.step, self.axis = step, self.left.index(step)
        sent = take(self.held, 1 - self.place[step], self.axis)
        bits = (None, ZHIGH, ZLOW, XBIT, CORE)
        self.got = swap(sent, bits[step]) if step else swap_rows(sent)

    def add(self):
        self.left.remove(self.step)
        kept = take(self.held, self.place[self.step], self.axis).astype(jnp.float32)
        kept = kept + self.got.astype(jnp.float32)
        self.held = kept.astype(jnp.bfloat16) if self.left else kept


def meet(values, chains):
    values, got = lax.optimization_barrier((values, [chain.got for chain in chains]))
    for chain, arrived in zip(chains, got):
        chain.got = arrived
        chain.add()
    return values


def heads_to_owners(attended, place):
    _, _, z_low, x_at, _ = place
    block = attended.shape[0] // 4
    own = attended[:block]
    x_part = swap(attended[block : 2 * block], XBIT)
    z_part = swap(attended[2 * block : 3 * block], ZLOW)
    far_part = swap(attended[3 * block :], XBIT | ZLOW)
    near = jnp.concatenate(pair(x_at, own, x_part), axis=1)
    far = jnp.concatenate(pair(x_at, z_part, far_part), axis=1)
    rows = jnp.concatenate(pair(z_low, near, far), axis=1)
    mine = block // 2
    return jnp.concatenate([rows[:mine], swap(rows[mine:], ZHIGH)])


def owners_to_heads(rows, place):
    _, _, z_low, x_at, _ = place
    mine = rows.shape[0] // 2
    rows = jnp.concatenate([rows[:mine], swap(rows[mine:], ZHIGH)])
    near, far = pair(z_low, rows[:, : 2 * GROUP], rows[:, 2 * GROUP :])
    own, x_part = pair(x_at, near[:, :GROUP], near[:, GROUP:])
    z_part, far_part = pair(x_at, far[:, :GROUP], far[:, GROUP:])
    return jnp.concatenate(
        [own, swap(x_part, XBIT), swap(z_part, ZLOW), swap(far_part, XBIT | ZLOW)]
    )


def local(
    tokens,
    segments,
    qkv_weight,
    out_weight,
    up_weight,
    down_weight,
    query_bias,
    value_bias,
    out_bias,
    first_gain,
    first_shift,
    up_bias,
    down_bias,
    second_gain,
    second_shift,
    cotangent,
):
    f32, low = jnp.float32, jnp.bfloat16
    width = tokens.shape[-1]
    shard = out_weight.shape[0]
    up_chunks = up_weight.shape[1] // width
    wide = up_chunks * shard
    vectors = (out_bias, first_gain, first_shift, down_bias, second_gain, second_shift)
    position = lax.axis_index("seq")
    z_high, z_low = position // 8, position // 4 % 2
    x_at, core = position // 2 % 2, position % 2
    place = (lax.axis_index("dp"), z_high, z_low, x_at, core)
    mine = z_high

    up_parts = up_weight.reshape(shard, up_chunks, width).transpose(1, 0, 2).reshape(wide, width)
    small, start = jnp.zeros((8, width), low), 0
    for vector in vectors + (up_bias,):
        ends = (start, width - start - vector.shape[0])
        small, start = small + jnp.pad(vector[None], ((0, 7), ends)), start + vector.shape[0]
    packed = jnp.concatenate([out_weight, up_parts, down_weight, small])
    gathered = lax.all_gather(packed, ("dp", "seq"), axis=0)

    group_tokens = gather_tokens(tokens, mine)
    all_segments = gather_segments(segments, mine)
    group_weight, query_b, value_b = gather_group_weight(
        qkv_weight, query_bias, value_bias, place
    )
    half = group_tokens.shape[0]
    query = jnp.dot(group_tokens, group_weight[:, :GROUP], preferred_element_type=f32)
    query = (query + query_b.astype(f32)).astype(low)
    key_value = jnp.dot(group_tokens, group_weight[:, GROUP:], preferred_element_type=f32)
    lift = jnp.concatenate([jnp.zeros((GROUP,), f32), value_b.astype(f32)])
    key_value = (key_value + lift).astype(low)
    key_value = jnp.concatenate([key_value, swap(key_value, CORE)])
    keys, values = key_value[:, :GROUP], key_value[:, GROUP:]
    segment_column = all_segments.reshape(-1, 1)
    attended_group, log_total = attend_group(
        query, keys, values, segment_column[:half], all_segments
    )
    attended = heads_to_owners(attended_group, place)

    out_full = gathered[:, :shard].reshape(-1, width)
    up_full = jnp.concatenate(
        [
            gathered[:, shard * (1 + at) : shard * (2 + at)].reshape(-1, width)
            for at in range(up_chunks)
        ],
        axis=1,
    )
    down_full = gathered[:, shard + wide : shard + 2 * wide].reshape(-1, width)
    flat = gathered[:, shard + 2 * wide].astype(f32)
    out_b, first_g, first_s, down_b, second_g, second_s = (
        flat[:, at * shard : (at + 1) * shard].reshape(-1) for at in range(len(vectors))
    )
    up_b = flat[:, 6 * shard : 6 * shard + wide].reshape(-1)

    inputs = jnp.concatenate([take(tokens, mine, 0), take(tokens, 1 - mine, 0)])
    branch = jnp.dot(attended, out_full, preferred_element_type=f32) + out_b
    normal1, scale1 = norm_parts(inputs.astype(f32) + branch)
    hidden = normal1 * first_g + first_s
    hidden_low = hidden.astype(low)
    inner = jnp.dot(hidden_low, up_full, preferred_element_type=f32) + up_b
    activated, gelu_pull = jax.vjp(exact_gelu, inner)
    activated_low = activated.astype(low)
    second = jnp.dot(activated_low, down_full, preferred_element_type=f32) + down_b
    normal2, scale2 = norm_parts(hidden + second)
    output = (normal2 * second_g + second_s).astype(low)
    output = jnp.stack(pair(mine, output[: output.shape[0] // 2], output[output.shape[0] // 2 :]))

    upstream = jnp.concatenate([take(cotangent, mine, 0), take(cotangent, 1 - mine, 0)])
    upstream = upstream.astype(f32)
    grad_sum2 = norm_back(upstream, normal2, scale2, second_g)
    grad_second = grad_sum2.astype(low)
    (grad_inner,) = gelu_pull(data_grad(grad_second, down_full))
    grad_inner = grad_inner.astype(low)
    grad_hidden = grad_sum2 + data_grad(grad_inner, up_full)
    grad_sum1 = norm_back(grad_hidden, normal1, scale1, first_g)
    grad_branch = grad_sum1.astype(low)
    grad_attended = data_grad(grad_branch, out_full).astype(low)

    grad_down = weight_grad(activated_low, grad_second).astype(low)
    grad_up = weight_grad(hidden_low, grad_inner).astype(low)
    grad_out = weight_grad(attended, grad_branch).astype(low)
    sums = (
        column_sum(grad_branch),
        jnp.sum(grad_hidden * normal1, axis=0),
        jnp.sum(grad_hidden, axis=0),
        column_sum(grad_second),
        jnp.sum(upstream * normal2, axis=0),
        jnp.sum(upstream, axis=0),
        column_sum(grad_inner),
    )
    sums = jnp.concatenate([item.reshape(32, -1) for item in sums], axis=1)
    sums = jnp.pad(sums[:, None], ((0, 0), (0, 7), (0, width - sums.shape[1]))).astype(low)
    rest = jnp.concatenate([grad_out.reshape(32, shard, width), sums], axis=1)
    at_dp, at_high, at_low, at_x, at_core = range(5)
    down = Chain(grad_down.reshape(32, wide, width), place)
    up = Chain(grad_up.reshape(32, shard, -1), place)
    rest = Chain(rest, place)
    chains = (down, up, rest)
    for chain in chains:
        chain.send(at_core)

    grad_group = owners_to_heads(grad_attended, place)
    grad_group = meet(grad_group, chains)
    down.send(at_x)
    up.send(at_dp)
    rest.send(at_low)
    attention = attend_group_back(
        query, keys, values, grad_group, log_total, all_segments[:, :half], segment_column
    )
    grad_query, grad_keys, grad_values = meet(attention, chains)
    down.send(at_dp)
    up.send(at_x)
    rest.send(at_x)
    grad_kv = jnp.concatenate([grad_keys, grad_values], axis=1)
    grad_kv = grad_kv[:half] + swap(grad_kv[half:].astype(low), CORE).astype(f32)
    grad_merged = jnp.concatenate([grad_query, grad_kv.astype(low)], axis=1)
    back = data_grad(grad_merged, group_weight)
    left_got, right_got = meet(scatter_first(back), chains)
    down.send(at_low)
    up.send(at_low)
    rest.send(at_dp)
    left, right, got = scatter_second(back, left_got, right_got)
    left, right, got = meet((left, right, got), chains)
    for chain in chains:
        chain.send(at_high)
    own_part, other_part = scatter_third(left, right, got)
    other_part = meet(other_part, chains).astype(f32)
    down_mine, up_mine, rest_mine = (chain.held for chain in chains)
    count = own_part.shape[0]
    own_grad = (grad_sum1[:count] + own_part).astype(low)
    other_grad = (grad_sum1[count:] + other_part).astype(low)
    input_grad = jnp.stack(pair(mine, own_grad, other_grad))
    grad_qkv, grad_query_bias, grad_value_bias = scatter_group_weight(
        weight_grad(group_tokens, grad_merged),
        column_sum(grad_merged[:, :GROUP]),
        column_sum(grad_merged[:, 2 * GROUP :]),
        place,
    )

    tail = rest_mine[shard]
    parts = [tail[at * shard : (at + 1) * shard] for at in range(6)]
    return (
        output,
        input_grad,
        grad_qkv,
        rest_mine[:shard],
        up_mine,
        down_mine,
        grad_query_bias,
        grad_value_bias,
        parts[0],
        parts[1],
        parts[2],
        tail[6 * shard : 6 * shard + wide],
        parts[3],
        parts[4],
        parts[5],
    )


def solution(mesh):
    in_specs = (
        P("dp", "seq", None),
        P("dp", "seq"),
        P(("dp", "seq"), None),
        P(("dp", "seq"), None),
        P(("dp", "seq"), None),
        P(("dp", "seq"), None),
        P(("dp", "seq")),
        P(("dp", "seq")),
        P(("dp", "seq")),
        P(("dp", "seq")),
        P(("dp", "seq")),
        P(("dp", "seq")),
        P(("dp", "seq")),
        P(("dp", "seq")),
        P(("dp", "seq")),
        P("dp", "seq", None),
    )
    out_specs = (
        P("dp", "seq", None),
        P("dp", "seq", None),
        P(("dp", "seq"), None),
        P(("dp", "seq"), None),
        P(("dp", "seq"), None),
        P(("dp", "seq"), None),
        P(("dp", "seq")),
        P(("dp", "seq")),
        P(("dp", "seq")),
        P(("dp", "seq")),
        P(("dp", "seq")),
        P(("dp", "seq")),
        P(("dp", "seq")),
        P(("dp", "seq")),
        P(("dp", "seq")),
    )
    fits = mesh.shape["dp"] == 2 and mesh.shape["seq"] == 16
    return jax.shard_map(
        local if fits else general_local, mesh=mesh, in_specs=in_specs, out_specs=out_specs, check_vma=False
    )
```

```python
import jax
import jax.numpy as jnp
from jax import lax
from jax.experimental import pallas as pl
from jax.experimental.pallas import tpu as pltpu
from jax.sharding import PartitionSpec as P

HEADS = 12
HEAD_DIM = 64
FF = 3072
DOC_MOST = 2000


EPS = 1e-12
NEGATIVE = -1e30


def norm_layer(summed, gain_row, shift_row):
    average = jnp.mean(summed, axis=-1, keepdims=True)
    centred = summed - average
    variance = jnp.mean(centred * centred, axis=-1, keepdims=True)
    return centred * lax.rsqrt(variance + EPS) * gain_row + shift_row


def exact_gelu(inner_rows):
    return jax.nn.gelu(inner_rows, approximate=False)


def same_value(state_pair):
    return state_pair


def head_split(matrix):
    return matrix.reshape(matrix.shape[0], HEADS, HEAD_DIM)


def block_scores(query_heads, key_rows):
    return (
        jnp.einsum(
            "qhd,khd->hqk", query_heads, head_split(key_rows), preferred_element_type=jnp.float32
        )
        * 0.125
    )


def probabilities(query_heads, key_stack, block_index, allowed, log_total):
    scores = block_scores(query_heads, key_stack[block_index, :, : HEADS * HEAD_DIM])
    return jnp.where(allowed[None], jnp.exp(scores - log_total[:, :, None]), 0.0)


def block_mask(query_segment, key_segments, block_index):
    return query_segment[:, None] == key_segments[block_index][None, :]


def log_totals(query_heads, key_stack, key_segments, query_segment):
    row_count = query_heads.shape[0]

    def log_visit(block_index, carry_state):
        allowed = block_mask(query_segment, key_segments, block_index)

        def log_compute(state_pair):
            top_now, total_now = state_pair
            scores = jnp.where(
                allowed[None],
                block_scores(query_heads, key_stack[block_index, :, : HEADS * HEAD_DIM]),
                NEGATIVE,
            )
            top_new = jnp.maximum(top_now, jnp.max(scores, axis=-1))
            expon_rows = jnp.where(allowed[None], jnp.exp(scores - top_new[:, :, None]), 0.0)
            return (top_new, total_now * jnp.exp(top_now - top_new) + jnp.sum(expon_rows, axis=-1))

        return lax.cond(jnp.any(allowed), log_compute, same_value, carry_state)

    initial = (
        jnp.full((HEADS, row_count), NEGATIVE, jnp.float32),
        jnp.zeros((HEADS, row_count), jnp.float32),
    )
    top_final, total_final = lax.fori_loop(0, key_stack.shape[0], log_visit, initial)
    return top_final + jnp.log(total_final)


def attend_values(query_heads, key_stack, key_segments, query_segment, log_total):
    model_width = HEADS * HEAD_DIM

    def attend_visit(block_index, running):
        allowed = block_mask(query_segment, key_segments, block_index)

        def attend_compute(running_in):
            main_sum, rest_sum = running_in
            weights_block = probabilities(query_heads, key_stack, block_index, allowed, log_total)
            weights_low = weights_block.astype(jnp.bfloat16)
            weights_rest = (weights_block - weights_low.astype(jnp.float32)).astype(jnp.bfloat16)
            value_heads = head_split(key_stack[block_index, :, model_width:])
            main_new = main_sum + jnp.einsum(
                "hqk,khd->qhd", weights_low, value_heads, preferred_element_type=jnp.float32
            )
            rest_new = rest_sum + jnp.einsum(
                "hqk,khd->qhd", weights_rest, value_heads, preferred_element_type=jnp.float32
            )
            return (main_new, rest_new)

        return lax.cond(jnp.any(allowed), attend_compute, same_value, running)

    zero_heads = jnp.zeros(query_heads.shape, jnp.float32)
    main_sum, rest_sum = lax.fori_loop(
        0, key_stack.shape[0], attend_visit, (zero_heads, zero_heads)
    )
    return (main_sum.reshape(query_heads.shape[0], model_width), main_sum + rest_sum)


def attention_back(
    query_heads, grad_heads, key_stack, key_segments, query_segment, log_total, exact_heads
):
    model_width = HEADS * HEAD_DIM
    row_count = query_heads.shape[0]
    delta_rows = jnp.einsum("qhd,qhd->hq", grad_heads.astype(jnp.float32), exact_heads)

    def grad_visit(block_index, carry_state):
        allowed = block_mask(query_segment, key_segments, block_index)

        def grad_compute(state_pair):
            grad_query_in, contrib_in = state_pair
            weights_block = probabilities(query_heads, key_stack, block_index, allowed, log_total)
            key_heads = head_split(key_stack[block_index, :, :model_width])
            value_heads = head_split(key_stack[block_index, :, model_width:])
            grad_probs = jnp.einsum(
                "qhd,khd->hqk", grad_heads, value_heads, preferred_element_type=jnp.float32
            )
            grad_scores = (weights_block * (grad_probs - delta_rows[:, :, None])).astype(
                jnp.bfloat16
            )
            grad_query_new = grad_query_in + jnp.einsum(
                "hqk,khd->qhd", grad_scores, key_heads, preferred_element_type=jnp.float32
            )
            grad_keys = (
                jnp.einsum(
                    "hqk,qhd->khd", grad_scores, query_heads, preferred_element_type=jnp.float32
                )
                * 0.125
            )
            grad_values = jnp.einsum(
                "hqk,qhd->khd",
                weights_block.astype(jnp.bfloat16),
                grad_heads,
                preferred_element_type=jnp.float32,
            )
            joined = jnp.concatenate(
                [
                    grad_keys.reshape(row_count, model_width),
                    grad_values.reshape(row_count, model_width),
                ],
                axis=1,
            )
            return (
                grad_query_new,
                lax.dynamic_update_index_in_dim(contrib_in, joined, block_index, 0),
            )

        return lax.cond(jnp.any(allowed), grad_compute, same_value, carry_state)

    initial = (
        jnp.zeros(query_heads.shape, jnp.float32),
        jnp.zeros((key_stack.shape[0], row_count, 2 * model_width), jnp.float32),
    )
    grad_query, contrib = lax.fori_loop(0, key_stack.shape[0], grad_visit, initial)
    return ((grad_query * 0.125).reshape(row_count, model_width), contrib)


def weight_grad(left_rows, right_rows):
    return jnp.einsum("rk,rn->kn", left_rows, right_rows, preferred_element_type=jnp.float32)


def data_grad(grad_rows, weight_full):
    return jnp.einsum("rn,kn->rk", grad_rows, weight_full, preferred_element_type=jnp.float32)


def column_sum(rows_low):
    return jnp.sum(rows_low.astype(jnp.float32), axis=0)


def general_local(
    tokens,
    segments,
    qkv_weight,
    out_weight,
    up_weight,
    down_weight,
    query_bias,
    value_bias,
    out_bias,
    first_gain,
    first_shift,
    up_bias,
    down_bias,
    second_gain,
    second_shift,
    cotangent,
):
    batch_count, row_count, model_width = tokens.shape
    seq_count = lax.axis_size("seq")
    reach = min((DOC_MOST + row_count - 2) // row_count, seq_count - 1)
    window = 2 * reach + 1
    position = lax.axis_index("seq")
    every_segment = lax.all_gather(segments, "seq", axis=1, tiled=True)
    padded_segment = jnp.pad(
        every_segment, ((0, 0), (reach * row_count, reach * row_count)), constant_values=-1
    )
    totals = [
        jnp.zeros((model_width, 3 * model_width), jnp.float32),
        jnp.zeros((model_width, model_width), jnp.float32),
        jnp.zeros((model_width, FF), jnp.float32),
        jnp.zeros((FF, model_width), jnp.float32),
        jnp.zeros((model_width,), jnp.float32),
        jnp.zeros((model_width,), jnp.float32),
        jnp.zeros((model_width,), jnp.float32),
        jnp.zeros((model_width,), jnp.float32),
        jnp.zeros((model_width,), jnp.float32),
        jnp.zeros((FF,), jnp.float32),
        jnp.zeros((model_width,), jnp.float32),
        jnp.zeros((model_width,), jnp.float32),
        jnp.zeros((model_width,), jnp.float32),
    ]
    outputs = []
    input_grads = []
    for micro in range(batch_count):
        weights_now = (
            lax.all_gather(qkv_weight, ("dp", "seq"), axis=0, tiled=True),
            lax.all_gather(out_weight, ("dp", "seq"), axis=0, tiled=True),
            lax.all_gather(up_weight, ("dp", "seq"), axis=0, tiled=True),
            lax.all_gather(down_weight, ("dp", "seq"), axis=0, tiled=True),
            lax.all_gather(query_bias, ("dp", "seq"), axis=0, tiled=True),
            lax.all_gather(value_bias, ("dp", "seq"), axis=0, tiled=True),
            lax.all_gather(out_bias, ("dp", "seq"), axis=0, tiled=True),
            lax.all_gather(first_gain, ("dp", "seq"), axis=0, tiled=True),
            lax.all_gather(first_shift, ("dp", "seq"), axis=0, tiled=True),
            lax.all_gather(up_bias, ("dp", "seq"), axis=0, tiled=True),
            lax.all_gather(down_bias, ("dp", "seq"), axis=0, tiled=True),
            lax.all_gather(second_gain, ("dp", "seq"), axis=0, tiled=True),
            lax.all_gather(second_shift, ("dp", "seq"), axis=0, tiled=True),
        )
        (
            qkv_full,
            out_full,
            up_full,
            down_full,
            query_b,
            value_b,
            out_b,
            first_g,
            first_s,
            up_b,
            down_b,
            second_g,
            second_s,
        ) = weights_now
        inputs = tokens[micro]
        merged = jnp.dot(inputs, qkv_full, preferred_element_type=jnp.float32)
        query = (merged[:, :model_width] + query_b.astype(jnp.float32)).astype(jnp.bfloat16)
        keys_now = merged[:, model_width : 2 * model_width].astype(jnp.bfloat16)
        values_now = (merged[:, 2 * model_width :] + value_b.astype(jnp.float32)).astype(
            jnp.bfloat16
        )
        whole_keys = lax.all_gather(
            jnp.concatenate([keys_now, values_now], axis=1), "seq", axis=0, tiled=True
        )
        padded = jnp.pad(whole_keys, ((reach * row_count, reach * row_count), (0, 0)))
        picked = lax.dynamic_slice_in_dim(padded, position * row_count, window * row_count, 0)
        key_stack = picked.reshape(window, row_count, 2 * model_width)
        key_segments = lax.dynamic_slice_in_dim(
            padded_segment[micro], position * row_count, window * row_count, 0
        ).reshape(window, row_count)
        query_segment = segments[micro]
        query_heads = head_split(query)
        log_total = log_totals(query_heads, key_stack, key_segments, query_segment)
        attended_f, exact_heads = attend_values(
            query_heads, key_stack, key_segments, query_segment, log_total
        )
        attended = attended_f.astype(jnp.bfloat16)
        branch = jnp.dot(attended, out_full, preferred_element_type=jnp.float32) + out_b.astype(
            jnp.float32
        )
        hidden, first_pull = jax.vjp(
            norm_layer,
            inputs.astype(jnp.float32) + branch,
            first_g.astype(jnp.float32),
            first_s.astype(jnp.float32),
        )
        hidden_low = hidden.astype(jnp.bfloat16)
        inner_rows = jnp.dot(hidden_low, up_full, preferred_element_type=jnp.float32) + up_b.astype(
            jnp.float32
        )
        activated, gelu_pull = jax.vjp(exact_gelu, inner_rows)
        activated_low = activated.astype(jnp.bfloat16)
        second = jnp.dot(
            activated_low, down_full, preferred_element_type=jnp.float32
        ) + down_b.astype(jnp.float32)
        output, second_pull = jax.vjp(
            norm_layer, hidden + second, second_g.astype(jnp.float32), second_s.astype(jnp.float32)
        )
        outputs.append(output.astype(jnp.bfloat16))
        back_weights = (
            lax.all_gather(qkv_weight, ("dp", "seq"), axis=0, tiled=True),
            lax.all_gather(out_weight, ("dp", "seq"), axis=0, tiled=True),
            lax.all_gather(up_weight, ("dp", "seq"), axis=0, tiled=True),
            lax.all_gather(down_weight, ("dp", "seq"), axis=0, tiled=True),
            lax.all_gather(query_bias, ("dp", "seq"), axis=0, tiled=True),
            lax.all_gather(value_bias, ("dp", "seq"), axis=0, tiled=True),
            lax.all_gather(out_bias, ("dp", "seq"), axis=0, tiled=True),
            lax.all_gather(first_gain, ("dp", "seq"), axis=0, tiled=True),
            lax.all_gather(first_shift, ("dp", "seq"), axis=0, tiled=True),
            lax.all_gather(up_bias, ("dp", "seq"), axis=0, tiled=True),
            lax.all_gather(down_bias, ("dp", "seq"), axis=0, tiled=True),
            lax.all_gather(second_gain, ("dp", "seq"), axis=0, tiled=True),
            lax.all_gather(second_shift, ("dp", "seq"), axis=0, tiled=True),
        )
        qkv_full, out_full, up_full, down_full = (
            back_weights[0],
            back_weights[1],
            back_weights[2],
            back_weights[3],
        )
        grad_sum2, grad_gain2, grad_shift2 = second_pull(cotangent[micro].astype(jnp.float32))
        grad_second = grad_sum2.astype(jnp.bfloat16)
        (grad_inner_f,) = gelu_pull(data_grad(grad_second, down_full))
        grad_inner = grad_inner_f.astype(jnp.bfloat16)
        grad_hidden = grad_sum2 + data_grad(grad_inner, up_full)
        grad_sum1, grad_gain1, grad_shift1 = first_pull(grad_hidden)
        grad_branch = grad_sum1.astype(jnp.bfloat16)
        grad_attended = data_grad(grad_branch, out_full).astype(jnp.bfloat16)
        grad_query_f, contrib = attention_back(
            query_heads,
            head_split(grad_attended),
            key_stack,
            key_segments,
            query_segment,
            log_total,
            exact_heads,
        )
        block_ids = position - reach + jnp.arange(window, dtype=jnp.int32)
        inside = (block_ids >= 0) & (block_ids < seq_count)
        canvas = jnp.zeros((seq_count, row_count, 2 * model_width), jnp.float32)
        canvas = canvas.at[jnp.clip(block_ids, 0, seq_count - 1)].add(
            jnp.where(inside[:, None, None], contrib, 0.0)
        )
        canvas = canvas.reshape(seq_count * row_count, 2 * model_width)
        key_value_grad = lax.psum_scatter(canvas, "seq", scatter_dimension=0, tiled=True)
        grad_query = grad_query_f.astype(jnp.bfloat16)
        grad_value = key_value_grad[:, model_width:].astype(jnp.bfloat16)
        grad_merged = jnp.concatenate(
            [grad_query, key_value_grad[:, :model_width].astype(jnp.bfloat16), grad_value], axis=1
        )
        input_grads.append((grad_sum1 + data_grad(grad_merged, qkv_full)).astype(jnp.bfloat16))
        terms = [
            weight_grad(inputs, grad_merged),
            weight_grad(attended, grad_branch),
            weight_grad(hidden_low, grad_inner),
            weight_grad(activated_low, grad_second),
            column_sum(grad_query),
            column_sum(grad_value),
            column_sum(grad_branch),
            grad_gain1,
            grad_shift1,
            column_sum(grad_inner),
            column_sum(grad_second),
            grad_gain2,
            grad_shift2,
        ]
        totals = [total_item + term_item for total_item, term_item in zip(totals, terms)]
    scattered = (
        lax.psum_scatter(totals[0], ("dp", "seq"), scatter_dimension=0, tiled=True),
        lax.psum_scatter(totals[1], ("dp", "seq"), scatter_dimension=0, tiled=True),
        lax.psum_scatter(totals[2], ("dp", "seq"), scatter_dimension=0, tiled=True),
        lax.psum_scatter(totals[3], ("dp", "seq"), scatter_dimension=0, tiled=True),
        lax.psum_scatter(totals[4], ("dp", "seq"), scatter_dimension=0, tiled=True),
        lax.psum_scatter(totals[5], ("dp", "seq"), scatter_dimension=0, tiled=True),
        lax.psum_scatter(totals[6], ("dp", "seq"), scatter_dimension=0, tiled=True),
        lax.psum_scatter(totals[7], ("dp", "seq"), scatter_dimension=0, tiled=True),
        lax.psum_scatter(totals[8], ("dp", "seq"), scatter_dimension=0, tiled=True),
        lax.psum_scatter(totals[9], ("dp", "seq"), scatter_dimension=0, tiled=True),
        lax.psum_scatter(totals[10], ("dp", "seq"), scatter_dimension=0, tiled=True),
        lax.psum_scatter(totals[11], ("dp", "seq"), scatter_dimension=0, tiled=True),
        lax.psum_scatter(totals[12], ("dp", "seq"), scatter_dimension=0, tiled=True),
    )
    return (
        jnp.stack(outputs),
        jnp.stack(input_grads),
        scattered[0],
        scattered[1],
        scattered[2],
        scattered[3],
        scattered[4],
        scattered[5],
        scattered[6],
        scattered[7],
        scattered[8],
        scattered[9],
        scattered[10],
        scattered[11],
        scattered[12],
    )


CORE, XBIT, ZLOW, ZHIGH = 1, 2, 4, 8
GROUPS = 4
GROUP = HEADS // GROUPS * HEAD_DIM
QROWS = 256


def swap(value, bit):
    return lax.ppermute(value, "seq", [(i, i ^ bit) for i in range(16)])


def swap_rows(value):
    return lax.ppermute(value, "dp", [(0, 1), (1, 0)])


def pair(bit, own, other):
    return jnp.where(bit == 0, own, other), jnp.where(bit == 0, other, own)


def join(bit, own, other, axis):
    return jnp.stack(pair(bit, own, other), axis=axis)


def take(value, index, axis):
    return lax.dynamic_index_in_dim(value, index, axis, keepdims=False)


def head_lanes(head, width):
    return lax.broadcasted_iota(jnp.int32, (1, width), 1) // HEAD_DIM == head


def attend_kernel(q_ref, k_ref, v_ref, qseg_ref, kseg_ref, out_ref, log_ref, bias_ref):
    width = q_ref.shape[1]
    rows = q_ref.shape[0]
    query = q_ref[...] * jnp.asarray(0.125, jnp.bfloat16)
    bias_ref[...] = jnp.where(qseg_ref[...] == kseg_ref[...], 0.0, NEGATIVE)
    total = jnp.zeros((rows, width), jnp.float32)
    for head in range(width // HEAD_DIM):
        lanes = head_lanes(head, width)
        masked = jnp.where(lanes, query, jnp.zeros_like(query))
        scores = lax.dot_general(
            masked, k_ref[...], (((1,), (1,)), ((), ())), preferred_element_type=jnp.float32
        )
        scores = scores + bias_ref[...]
        top = jnp.max(scores, axis=1, keepdims=True)
        expon = jnp.exp(scores - top)
        norm = jnp.sum(expon, axis=1, keepdims=True)
        value = jnp.dot(
            expon.astype(jnp.bfloat16), v_ref[...], preferred_element_type=jnp.float32
        )
        log_rows = jnp.transpose(jnp.broadcast_to(top + jnp.log(norm), (rows, 128)))
        log_ref[head : head + 1, :] = log_rows[0:1]
        total = total + jnp.where(lanes, value / norm, 0.0)
    out_ref[...] = total.astype(jnp.bfloat16)


def attend_group(query, keys, values, qseg_column, kseg_row):
    rows, width = query.shape
    count = keys.shape[0]
    return pl.pallas_call(
        attend_kernel,
        grid=(rows // QROWS,),
        in_specs=[
            pl.BlockSpec((QROWS, width), lambda i: (i, 0)),
            pl.BlockSpec((count, width), lambda i: (0, 0)),
            pl.BlockSpec((count, width), lambda i: (0, 0)),
            pl.BlockSpec((QROWS, 1), lambda i: (i, 0)),
            pl.BlockSpec((1, count), lambda i: (0, 0)),
        ],
        out_specs=[
            pl.BlockSpec((QROWS, width), lambda i: (i, 0)),
            pl.BlockSpec((8, QROWS), lambda i: (0, i)),
        ],
        out_shape=[
            jax.ShapeDtypeStruct((rows, width), jnp.bfloat16),
            jax.ShapeDtypeStruct((8, rows), jnp.float32),
        ],
        scratch_shapes=[pltpu.VMEM((QROWS, count), jnp.float32)],
        cost_estimate=pl.CostEstimate(
            flops=4 * rows * count * 256 * (width // HEAD_DIM),
            bytes_accessed=4 * (rows + count) * width,
            transcendentals=rows * count * (width // HEAD_DIM),
        ),
        compiler_params=pltpu.CompilerParams(vmem_limit_bytes=60 * 1024 * 1024),
    )(query, keys, values, qseg_column, kseg_row)


def attend_back_kernel(
    q_ref, k_ref, v_ref, grad_ref, log_ref, qseg_ref, kseg_ref, dq_ref, dk_ref, dv_ref, bias_ref
):
    width = q_ref.shape[1]
    query = q_ref[...] * jnp.asarray(0.125, jnp.bfloat16)
    grad = grad_ref[...]
    bias_ref[...] = jnp.where(kseg_ref[...] == qseg_ref[...], 0.0, NEGATIVE)

    @pl.when(pl.program_id(0) == 0)
    def clear():
        dk_ref[...] = jnp.zeros_like(dk_ref)
        dv_ref[...] = jnp.zeros_like(dv_ref)

    total = jnp.zeros(query.shape, jnp.float32)
    for head in range(width // HEAD_DIM):
        lanes = head_lanes(head, width)
        query_now = jnp.where(lanes, query, jnp.zeros_like(query))
        grad_now = jnp.where(lanes, grad, jnp.zeros_like(grad))
        scores = lax.dot_general(
            k_ref[...], query_now, (((1,), (1,)), ((), ())), preferred_element_type=jnp.float32
        )
        prob = jnp.exp(scores + bias_ref[...] - log_ref[head : head + 1, :])
        grad_prob = lax.dot_general(
            v_ref[...], grad_now, (((1,), (1,)), ((), ())), preferred_element_type=jnp.float32
        )
        delta = jnp.sum(prob * grad_prob, axis=0, keepdims=True)
        grad_score = (prob * (grad_prob - delta)).astype(jnp.bfloat16)
        dv_ref[...] += jnp.dot(
            prob.astype(jnp.bfloat16), grad_now, preferred_element_type=jnp.float32
        )
        dk_ref[...] += jnp.dot(grad_score, query_now, preferred_element_type=jnp.float32)
        dq = lax.dot_general(
            grad_score, k_ref[...], (((0,), (0,)), ((), ())), preferred_element_type=jnp.float32
        )
        total = total + jnp.where(lanes, dq * 0.125, 0.0)
    dq_ref[...] = total.astype(jnp.bfloat16)


def attend_group_back(query, keys, values, grad, log_total, qseg_row, kseg_column):
    rows, width = query.shape
    count = keys.shape[0]
    return pl.pallas_call(
        attend_back_kernel,
        grid=(rows // QROWS,),
        in_specs=[
            pl.BlockSpec((QROWS, width), lambda i: (i, 0)),
            pl.BlockSpec((count, width), lambda i: (0, 0)),
            pl.BlockSpec((count, width), lambda i: (0, 0)),
            pl.BlockSpec((QROWS, width), lambda i: (i, 0)),
            pl.BlockSpec((8, QROWS), lambda i: (0, i)),
            pl.BlockSpec((1, QROWS), lambda i: (0, i)),
            pl.BlockSpec((count, 1), lambda i: (0, 0)),
        ],
        out_specs=[
            pl.BlockSpec((QROWS, width), lambda i: (i, 0)),
            pl.BlockSpec((count, width), lambda i: (0, 0)),
            pl.BlockSpec((count, width), lambda i: (0, 0)),
        ],
        out_shape=[
            jax.ShapeDtypeStruct((rows, width), jnp.bfloat16),
            jax.ShapeDtypeStruct((count, width), jnp.float32),
            jax.ShapeDtypeStruct((count, width), jnp.float32),
        ],
        scratch_shapes=[pltpu.VMEM((count, QROWS), jnp.float32)],
        cost_estimate=pl.CostEstimate(
            flops=10 * rows * count * 256 * (width // HEAD_DIM),
            bytes_accessed=8 * (rows + count) * width,
            transcendentals=rows * count * (width // HEAD_DIM),
        ),
        compiler_params=pltpu.CompilerParams(vmem_limit_bytes=60 * 1024 * 1024),
    )(query, keys, values, grad, log_total, qseg_row, kseg_column)


def norm_parts(summed):
    centred = summed - jnp.mean(summed, axis=-1, keepdims=True)
    scale = lax.rsqrt(jnp.mean(centred * centred, axis=-1, keepdims=True) + EPS)
    return centred * scale, scale


def norm_back(grad, normal, scale, gain):
    grad_normal = grad * gain
    inside = grad_normal - jnp.mean(grad_normal, axis=-1, keepdims=True)
    return scale * (inside - normal * jnp.mean(grad_normal * normal, axis=-1, keepdims=True))


def gather_tokens(tokens, seq_mine):
    first = jnp.concatenate(
        [take(tokens, seq_mine, 0), swap(take(tokens, 1 - seq_mine, 0), ZHIGH)]
    )
    half = tokens.shape[-1] // 2
    block = first.shape[0]
    left, right = first[:, :half], first[:, half:]
    left_two = jnp.concatenate([left, swap(left, XBIT)])
    right_z = swap(right, ZLOW)
    left_far = swap(left_two, ZLOW)
    right_far = swap(jnp.concatenate([right, right_z]), XBIT)
    right_four = jnp.concatenate([right, right_far[:block], right_z, right_far[block:]])
    return jnp.concatenate([jnp.concatenate([left_two, left_far]), right_four], axis=1)


def gather_segments(segments, seq_mine):
    held = jnp.concatenate(
        [take(segments, seq_mine, 0), swap(take(segments, 1 - seq_mine, 0), ZHIGH)]
    ).reshape(1, -1)
    held = jnp.concatenate([held, swap(held, XBIT)], axis=1)
    held = jnp.concatenate([held, swap(held, ZLOW)], axis=1)
    return jnp.concatenate([held, swap(held, CORE)], axis=1)


def add_pair(one, other):
    return one.astype(jnp.float32) + other.astype(jnp.float32)


def scatter_first(partial):
    block = partial.shape[0] // 4
    low = partial.astype(jnp.bfloat16)
    return (
        swap(low[3 * block :], XBIT | ZLOW),
        swap(low[block : 2 * block], XBIT),
        swap(low[2 * block : 3 * block], ZLOW),
    )


def scatter_second(partial, got):
    block = partial.shape[0] // 4
    total = partial[:block] + add_pair(got[0], got[1]) + got[2].astype(jnp.float32)
    mine = block // 2
    return total[:mine], swap(total[mine:].astype(jnp.bfloat16), ZHIGH)


def gather_group_weight(weight, query_bias, value_bias, place):
    dp_at, z_high, z_low, x_at, core = place
    rows = weight.shape[0]
    pieces = weight.reshape(rows, 3, 2, 2, GROUP).transpose(2, 3, 0, 1, 4)
    pieces = pieces.reshape(2, 2, rows, 3 * GROUP)
    biases = jnp.concatenate([query_bias, value_bias])
    extra = jnp.pad(biases[None], ((0, 7), (0, 3 * GROUP - biases.shape[0])))
    extra = jnp.broadcast_to(extra[None, None], (2, 2) + extra.shape)
    pieces = jnp.concatenate([pieces, extra], axis=2)
    held = join(x_at, take(pieces, x_at, 1), swap(take(pieces, 1 - x_at, 1), XBIT), 0)
    held = join(z_low, take(held, z_low, 1), swap(take(held, 1 - z_low, 1), ZLOW), 0)
    held = join(z_high, held, swap(held, ZHIGH), 0)
    held = join(dp_at, held, swap_rows(held), 0)
    held = join(core, held, swap(held, CORE), 4)
    held = held.reshape(32, rows + 8, 3 * GROUP)
    group = z_low * 2 + x_at
    query_full = held[:, rows, :rows].reshape(-1)
    value_full = held[:, rows, rows : 2 * rows].reshape(-1)
    return (
        held[:, :rows].reshape(32 * rows, 3 * GROUP),
        take(query_full.reshape(GROUPS, GROUP), group, 0),
        take(value_full.reshape(GROUPS, GROUP), group, 0),
    )


def swap_any(value, bits):
    return lax.ppermute(value, ("dp", "seq"), [(i, i ^ bits) for i in range(32)])


class GroupChain:
    def __init__(self, grad, query_sums, value_sums, place):
        dp_at, z_high, z_low, x_at, core = self.place = place
        self.rows = rows = grad.shape[0] // 32
        group = z_low * 2 + x_at
        sums = jnp.concatenate([query_sums.reshape(8, rows), value_sums.reshape(8, rows)], axis=1)
        owner = jnp.arange(32, dtype=jnp.int32)[:, None] // 8 == group
        sums = jnp.where(owner, jnp.tile(sums, (4, 1)), 0.0)
        extra = jnp.pad(sums[:, None], ((0, 0), (0, 7), (0, 3 * GROUP - 2 * rows)))
        held = jnp.concatenate([grad.reshape(32, rows, 3 * GROUP), extra], axis=1)
        self.shape = held.shape[1:]
        held = held.astype(jnp.bfloat16).reshape((16, 2) + self.shape)
        self.kept = take(held, core, 1)
        self.got = swap(take(held, 1 - core, 1), CORE)

    def next(self):
        dp_at, z_high = self.place[:2]
        held = add_pair(self.kept, self.got).astype(jnp.bfloat16).reshape((4, 4) + self.shape)
        at = dp_at * 2 + z_high
        self.kept = take(held, at, 0)
        self.got = [
            swap_any(take(held, at ^ other, 0), bits)
            for other, bits in ((3, 16 | ZHIGH), (2, 16), (1, ZHIGH))
        ]

    def last(self):
        _, _, z_low, x_at, _ = self.place
        held = add_pair(self.kept, self.got[0]) + add_pair(self.got[1], self.got[2])
        held = held.astype(jnp.bfloat16)
        at = z_low * 2 + x_at
        self.kept = take(held, at, 0)
        self.got = [
            swap(take(held, at ^ other, 0), bits)
            for other, bits in ((3, XBIT | ZLOW), (2, ZLOW), (1, XBIT))
        ]

    def result(self):
        _, _, z_low, x_at, _ = self.place
        far, z_part, x_part = self.got
        near, other = pair(x_at, self.kept, x_part), pair(x_at, z_part, far)
        low, high = zip(*(pair(z_low, one, two) for one, two in zip(near, other)))
        held = jnp.stack(low + high).astype(jnp.float32)
        rows = self.rows
        weight = held[:, :rows].reshape(GROUPS, rows, 3, GROUP).transpose(1, 2, 0, 3)
        biases = jnp.sum(held[:, rows, : 2 * rows], axis=0)
        return weight.reshape(rows, 3 * GROUPS * GROUP), biases[:rows], biases[rows:]


class Chain:
    def __init__(self, held, place):
        self.place = place
        self.left = list(range(5))
        self.rows, self.columns = held.shape[1:]
        self.held = held.reshape(32 * self.rows, self.columns)

    def half(self, at):
        before = 2**self.axis
        split = self.held.reshape(before, 2, -1, self.columns)
        return take(split, at, 1).reshape(-1, self.columns)

    def send(self, step):
        self.step, self.axis = step, self.left.index(step)
        bits = (None, ZHIGH, ZLOW, XBIT, CORE)
        sent = self.half(1 - self.place[step])
        self.got = swap(sent, bits[step]) if step else swap_rows(sent)

    def add(self):
        self.left.remove(self.step)
        kept = self.half(self.place[self.step]).astype(jnp.float32)
        kept = kept + self.got.astype(jnp.float32)
        self.held = kept.astype(jnp.bfloat16) if self.left else kept


def meet(values, chains):
    values, got = lax.optimization_barrier((values, [chain.got for chain in chains]))
    for chain, arrived in zip(chains, got):
        chain.got = arrived
        chain.add()
    return values


def heads_to_owners(attended, place):
    _, _, z_low, x_at, _ = place
    block = attended.shape[0] // 4
    own = attended[:block]
    x_part = swap(attended[block : 2 * block], XBIT)
    z_part = swap(attended[2 * block : 3 * block], ZLOW)
    far_part = swap(attended[3 * block :], XBIT | ZLOW)
    near = jnp.concatenate(pair(x_at, own, x_part), axis=1)
    far = jnp.concatenate(pair(x_at, z_part, far_part), axis=1)
    rows = jnp.concatenate(pair(z_low, near, far), axis=1)
    mine = block // 2
    return jnp.concatenate([rows[:mine], swap(rows[mine:], ZHIGH)])


def owners_to_rows(rows):
    mine = rows.shape[0] // 2
    return jnp.concatenate([rows[:mine], swap(rows[mine:], ZHIGH)])


def rows_to_heads(rows, place):
    _, _, z_low, x_at, _ = place
    near, far = pair(z_low, rows[:, : 2 * GROUP], rows[:, 2 * GROUP :])
    own, x_part = pair(x_at, near[:, :GROUP], near[:, GROUP:])
    z_part, far_part = pair(x_at, far[:, :GROUP], far[:, GROUP:])
    return jnp.concatenate(
        [own, swap(x_part, XBIT), swap(z_part, ZLOW), swap(far_part, XBIT | ZLOW)]
    )


def local(
    tokens,
    segments,
    qkv_weight,
    out_weight,
    up_weight,
    down_weight,
    query_bias,
    value_bias,
    out_bias,
    first_gain,
    first_shift,
    up_bias,
    down_bias,
    second_gain,
    second_shift,
    cotangent,
):
    f32, low = jnp.float32, jnp.bfloat16
    width = tokens.shape[-1]
    shard = out_weight.shape[0]
    up_chunks = up_weight.shape[1] // width
    wide = up_chunks * shard
    vectors = (out_bias, first_gain, first_shift, down_bias, second_gain, second_shift)
    position = lax.axis_index("seq")
    z_high, z_low = position // 8, position // 4 % 2
    x_at, core = position // 2 % 2, position % 2
    place = (lax.axis_index("dp"), z_high, z_low, x_at, core)
    mine = z_high

    up_parts = up_weight.reshape(shard, up_chunks, width).transpose(1, 0, 2).reshape(wide, width)
    small, start = jnp.zeros((8, width), low), 0
    for vector in vectors + (up_bias,):
        ends = (start, width - start - vector.shape[0])
        small, start = small + jnp.pad(vector[None], ((0, 7), ends)), start + vector.shape[0]
    packed = jnp.concatenate([out_weight, up_parts, down_weight, small])
    gathered = lax.all_gather(packed, ("dp", "seq"), axis=0)

    group_tokens = gather_tokens(tokens, mine)
    all_segments = gather_segments(segments, mine)
    group_weight, query_b, value_b = gather_group_weight(
        qkv_weight, query_bias, value_bias, place
    )
    half = group_tokens.shape[0]
    query = jnp.dot(group_tokens, group_weight[:, :GROUP], preferred_element_type=f32)
    query = (query + query_b.astype(f32)).astype(low)
    key_value = jnp.dot(group_tokens, group_weight[:, GROUP:], preferred_element_type=f32)
    lift = jnp.concatenate([jnp.zeros((GROUP,), f32), value_b.astype(f32)])
    key_value = (key_value + lift).astype(low)
    key_value = jnp.concatenate([key_value, swap(key_value, CORE)])
    keys, values = key_value[:, :GROUP], key_value[:, GROUP:]
    segment_column = all_segments.reshape(-1, 1)
    attended_group, log_total = attend_group(
        query, keys, values, segment_column[:half], all_segments
    )
    attended = heads_to_owners(attended_group, place)

    out_full = gathered[:, :shard].reshape(-1, width)
    up_full = jnp.concatenate(
        [
            gathered[:, shard * (1 + at) : shard * (2 + at)].reshape(-1, width)
            for at in range(up_chunks)
        ],
        axis=1,
    )
    down_full = gathered[:, shard + wide : shard + 2 * wide].reshape(-1, width)
    flat = gathered[:, shard + 2 * wide].astype(f32)
    out_b, first_g, first_s, down_b, second_g, second_s = (
        flat[:, at * shard : (at + 1) * shard].reshape(-1) for at in range(len(vectors))
    )
    up_b = flat[:, 6 * shard : 6 * shard + wide].reshape(-1)

    inputs = jnp.concatenate([take(tokens, mine, 0), take(tokens, 1 - mine, 0)])
    branch = jnp.dot(attended, out_full, preferred_element_type=f32) + out_b
    normal1, scale1 = norm_parts(inputs.astype(f32) + branch)
    hidden = normal1 * first_g + first_s
    hidden_low = hidden.astype(low)
    inner = jnp.dot(hidden_low, up_full, preferred_element_type=f32) + up_b
    activated, gelu_pull = jax.vjp(exact_gelu, inner)
    activated_low = activated.astype(low)
    second = jnp.dot(activated_low, down_full, preferred_element_type=f32) + down_b
    normal2, scale2 = norm_parts(hidden + second)
    output = (normal2 * second_g + second_s).astype(low)
    output = jnp.stack(pair(mine, output[: output.shape[0] // 2], output[output.shape[0] // 2 :]))

    upstream = jnp.concatenate([take(cotangent, mine, 0), take(cotangent, 1 - mine, 0)])
    upstream = upstream.astype(f32)
    grad_sum2 = norm_back(upstream, normal2, scale2, second_g)
    grad_second = grad_sum2.astype(low)
    (grad_inner,) = gelu_pull(data_grad(grad_second, down_full))
    grad_inner = grad_inner.astype(low)
    grad_hidden = grad_sum2 + data_grad(grad_inner, up_full)
    grad_sum1 = norm_back(grad_hidden, normal1, scale1, first_g)
    grad_branch = grad_sum1.astype(low)
    grad_attended = data_grad(grad_branch, out_full).astype(low)
    grad_rows = owners_to_rows(grad_attended)
    _, activated_low = lax.optimization_barrier((grad_attended, activated_low))
    grad_rows, hidden_low, attended = lax.optimization_barrier((grad_rows, hidden_low, attended))

    grad_down = weight_grad(activated_low, grad_second).astype(low)
    grad_up = weight_grad(hidden_low, grad_inner).astype(low)
    grad_out = weight_grad(attended, grad_branch).astype(low)
    sums = (
        column_sum(grad_branch),
        jnp.sum(grad_hidden * normal1, axis=0),
        jnp.sum(grad_hidden, axis=0),
        column_sum(grad_second),
        jnp.sum(upstream * normal2, axis=0),
        jnp.sum(upstream, axis=0),
        column_sum(grad_inner),
    )
    sums = jnp.concatenate([item.reshape(32, -1) for item in sums], axis=1)
    sums = jnp.pad(sums[:, None], ((0, 0), (0, 7), (0, width - sums.shape[1]))).astype(low)
    rest = jnp.concatenate([grad_out.reshape(32, shard, width), sums], axis=1)
    at_dp, at_high, at_low, at_x, at_core = range(5)
    down = Chain(grad_down.reshape(32, wide, width), place)
    up = Chain(grad_up.reshape(32, shard, -1), place)
    rest = Chain(rest, place)
    chains = (down, up, rest)
    for chain in chains:
        chain.send(at_core)

    grad_group = rows_to_heads(grad_rows, place)
    grad_group = meet(grad_group, chains)
    down.send(at_x)
    up.send(at_dp)
    rest.send(at_low)
    attention = attend_group_back(
        query, keys, values, grad_group, log_total, all_segments[:, :half], segment_column
    )
    grad_query, grad_keys, grad_values = meet(attention, chains)
    down.send(at_dp)
    up.send(at_high)
    rest.send(at_x)
    grad_kv = jnp.concatenate([grad_keys, grad_values], axis=1)
    grad_kv = grad_kv[:half] + swap(grad_kv[half:].astype(low), CORE).astype(f32)
    grad_merged = jnp.concatenate([grad_query, grad_kv.astype(low)], axis=1)
    back = data_grad(grad_merged, group_weight)
    back_got = scatter_first(back)
    group_chain = GroupChain(
        weight_grad(group_tokens, grad_merged),
        column_sum(grad_merged[:, :GROUP]),
        column_sum(grad_merged[:, 2 * GROUP :]),
        place,
    )
    back_got, group_chain.got = meet((back_got, group_chain.got), chains)
    own_part, other_part = scatter_second(back, back_got)
    group_chain.next()
    down.send(at_high)
    up.send(at_x)
    rest.send(at_dp)
    other_part, group_chain.got = meet((other_part, group_chain.got), chains)
    group_chain.last()
    down.send(at_low)
    up.send(at_low)
    rest.send(at_high)
    group_chain.got = meet(group_chain.got, chains)
    down_mine, up_mine, rest_mine = (chain.held for chain in chains)
    other_part = other_part.astype(f32)
    count = own_part.shape[0]
    own_grad = (grad_sum1[:count] + own_part).astype(low)
    other_grad = (grad_sum1[count:] + other_part).astype(low)
    input_grad = jnp.stack(pair(mine, own_grad, other_grad))
    grad_qkv, grad_query_bias, grad_value_bias = group_chain.result()

    tail = rest_mine[shard]
    parts = [tail[at * shard : (at + 1) * shard] for at in range(6)]
    return (
        output,
        input_grad,
        grad_qkv,
        rest_mine[:shard],
        up_mine,
        down_mine,
        grad_query_bias,
        grad_value_bias,
        parts[0],
        parts[1],
        parts[2],
        tail[6 * shard : 6 * shard + wide],
        parts[3],
        parts[4],
        parts[5],
    )


def solution(mesh):
    in_specs = (
        P("dp", "seq", None),
        P("dp", "seq"),
        P(("dp", "seq"), None),
        P(("dp", "seq"), None),
        P(("dp", "seq"), None),
        P(("dp", "seq"), None),
        P(("dp", "seq")),
        P(("dp", "seq")),
        P(("dp", "seq")),
        P(("dp", "seq")),
        P(("dp", "seq")),
        P(("dp", "seq")),
        P(("dp", "seq")),
        P(("dp", "seq")),
        P(("dp", "seq")),
        P("dp", "seq", None),
    )
    out_specs = (
        P("dp", "seq", None),
        P("dp", "seq", None),
        P(("dp", "seq"), None),
        P(("dp", "seq"), None),
        P(("dp", "seq"), None),
        P(("dp", "seq"), None),
        P(("dp", "seq")),
        P(("dp", "seq")),
        P(("dp", "seq")),
        P(("dp", "seq")),
        P(("dp", "seq")),
        P(("dp", "seq")),
        P(("dp", "seq")),
        P(("dp", "seq")),
        P(("dp", "seq")),
    )
    fits = mesh.shape["dp"] == 2 and mesh.shape["seq"] == 16
    return jax.shard_map(
        local if fits else general_local, mesh=mesh, in_specs=in_specs, out_specs=out_specs, check_vma=False
    )
```

```python
import jax
import jax.numpy as jnp
from jax import lax
from jax.experimental import pallas as pl
from jax.experimental.pallas import tpu as pltpu
from jax.sharding import PartitionSpec as P

HEADS = 12
HEAD_DIM = 64
FF = 3072
DOC_MOST = 2000


EPS = 1e-12
NEGATIVE = -1e30


def norm_layer(summed, gain_row, shift_row):
    average = jnp.mean(summed, axis=-1, keepdims=True)
    centred = summed - average
    variance = jnp.mean(centred * centred, axis=-1, keepdims=True)
    return centred * lax.rsqrt(variance + EPS) * gain_row + shift_row


def exact_gelu(inner_rows):
    return jax.nn.gelu(inner_rows, approximate=False)


def same_value(state_pair):
    return state_pair


def head_split(matrix):
    return matrix.reshape(matrix.shape[0], HEADS, HEAD_DIM)


def block_scores(query_heads, key_rows):
    return (
        jnp.einsum(
            "qhd,khd->hqk", query_heads, head_split(key_rows), preferred_element_type=jnp.float32
        )
        * 0.125
    )


def probabilities(query_heads, key_stack, block_index, allowed, log_total):
    scores = block_scores(query_heads, key_stack[block_index, :, : HEADS * HEAD_DIM])
    return jnp.where(allowed[None], jnp.exp(scores - log_total[:, :, None]), 0.0)


def block_mask(query_segment, key_segments, block_index):
    return query_segment[:, None] == key_segments[block_index][None, :]


def log_totals(query_heads, key_stack, key_segments, query_segment):
    row_count = query_heads.shape[0]

    def log_visit(block_index, carry_state):
        allowed = block_mask(query_segment, key_segments, block_index)

        def log_compute(state_pair):
            top_now, total_now = state_pair
            scores = jnp.where(
                allowed[None],
                block_scores(query_heads, key_stack[block_index, :, : HEADS * HEAD_DIM]),
                NEGATIVE,
            )
            top_new = jnp.maximum(top_now, jnp.max(scores, axis=-1))
            expon_rows = jnp.where(allowed[None], jnp.exp(scores - top_new[:, :, None]), 0.0)
            return (top_new, total_now * jnp.exp(top_now - top_new) + jnp.sum(expon_rows, axis=-1))

        return lax.cond(jnp.any(allowed), log_compute, same_value, carry_state)

    initial = (
        jnp.full((HEADS, row_count), NEGATIVE, jnp.float32),
        jnp.zeros((HEADS, row_count), jnp.float32),
    )
    top_final, total_final = lax.fori_loop(0, key_stack.shape[0], log_visit, initial)
    return top_final + jnp.log(total_final)


def attend_values(query_heads, key_stack, key_segments, query_segment, log_total):
    model_width = HEADS * HEAD_DIM

    def attend_visit(block_index, running):
        allowed = block_mask(query_segment, key_segments, block_index)

        def attend_compute(running_in):
            main_sum, rest_sum = running_in
            weights_block = probabilities(query_heads, key_stack, block_index, allowed, log_total)
            weights_low = weights_block.astype(jnp.bfloat16)
            weights_rest = (weights_block - weights_low.astype(jnp.float32)).astype(jnp.bfloat16)
            value_heads = head_split(key_stack[block_index, :, model_width:])
            main_new = main_sum + jnp.einsum(
                "hqk,khd->qhd", weights_low, value_heads, preferred_element_type=jnp.float32
            )
            rest_new = rest_sum + jnp.einsum(
                "hqk,khd->qhd", weights_rest, value_heads, preferred_element_type=jnp.float32
            )
            return (main_new, rest_new)

        return lax.cond(jnp.any(allowed), attend_compute, same_value, running)

    zero_heads = jnp.zeros(query_heads.shape, jnp.float32)
    main_sum, rest_sum = lax.fori_loop(
        0, key_stack.shape[0], attend_visit, (zero_heads, zero_heads)
    )
    return (main_sum.reshape(query_heads.shape[0], model_width), main_sum + rest_sum)


def attention_back(
    query_heads, grad_heads, key_stack, key_segments, query_segment, log_total, exact_heads
):
    model_width = HEADS * HEAD_DIM
    row_count = query_heads.shape[0]
    delta_rows = jnp.einsum("qhd,qhd->hq", grad_heads.astype(jnp.float32), exact_heads)

    def grad_visit(block_index, carry_state):
        allowed = block_mask(query_segment, key_segments, block_index)

        def grad_compute(state_pair):
            grad_query_in, contrib_in = state_pair
            weights_block = probabilities(query_heads, key_stack, block_index, allowed, log_total)
            key_heads = head_split(key_stack[block_index, :, :model_width])
            value_heads = head_split(key_stack[block_index, :, model_width:])
            grad_probs = jnp.einsum(
                "qhd,khd->hqk", grad_heads, value_heads, preferred_element_type=jnp.float32
            )
            grad_scores = (weights_block * (grad_probs - delta_rows[:, :, None])).astype(
                jnp.bfloat16
            )
            grad_query_new = grad_query_in + jnp.einsum(
                "hqk,khd->qhd", grad_scores, key_heads, preferred_element_type=jnp.float32
            )
            grad_keys = (
                jnp.einsum(
                    "hqk,qhd->khd", grad_scores, query_heads, preferred_element_type=jnp.float32
                )
                * 0.125
            )
            grad_values = jnp.einsum(
                "hqk,qhd->khd",
                weights_block.astype(jnp.bfloat16),
                grad_heads,
                preferred_element_type=jnp.float32,
            )
            joined = jnp.concatenate(
                [
                    grad_keys.reshape(row_count, model_width),
                    grad_values.reshape(row_count, model_width),
                ],
                axis=1,
            )
            return (
                grad_query_new,
                lax.dynamic_update_index_in_dim(contrib_in, joined, block_index, 0),
            )

        return lax.cond(jnp.any(allowed), grad_compute, same_value, carry_state)

    initial = (
        jnp.zeros(query_heads.shape, jnp.float32),
        jnp.zeros((key_stack.shape[0], row_count, 2 * model_width), jnp.float32),
    )
    grad_query, contrib = lax.fori_loop(0, key_stack.shape[0], grad_visit, initial)
    return ((grad_query * 0.125).reshape(row_count, model_width), contrib)


def weight_grad(left_rows, right_rows):
    return jnp.einsum("rk,rn->kn", left_rows, right_rows, preferred_element_type=jnp.float32)


def data_grad(grad_rows, weight_full):
    return jnp.einsum("rn,kn->rk", grad_rows, weight_full, preferred_element_type=jnp.float32)


def column_sum(rows_low):
    return jnp.sum(rows_low.astype(jnp.float32), axis=0)


def general_local(
    tokens,
    segments,
    qkv_weight,
    out_weight,
    up_weight,
    down_weight,
    query_bias,
    value_bias,
    out_bias,
    first_gain,
    first_shift,
    up_bias,
    down_bias,
    second_gain,
    second_shift,
    cotangent,
):
    batch_count, row_count, model_width = tokens.shape
    seq_count = lax.axis_size("seq")
    reach = min((DOC_MOST + row_count - 2) // row_count, seq_count - 1)
    window = 2 * reach + 1
    position = lax.axis_index("seq")
    every_segment = lax.all_gather(segments, "seq", axis=1, tiled=True)
    padded_segment = jnp.pad(
        every_segment, ((0, 0), (reach * row_count, reach * row_count)), constant_values=-1
    )
    totals = [
        jnp.zeros((model_width, 3 * model_width), jnp.float32),
        jnp.zeros((model_width, model_width), jnp.float32),
        jnp.zeros((model_width, FF), jnp.float32),
        jnp.zeros((FF, model_width), jnp.float32),
        jnp.zeros((model_width,), jnp.float32),
        jnp.zeros((model_width,), jnp.float32),
        jnp.zeros((model_width,), jnp.float32),
        jnp.zeros((model_width,), jnp.float32),
        jnp.zeros((model_width,), jnp.float32),
        jnp.zeros((FF,), jnp.float32),
        jnp.zeros((model_width,), jnp.float32),
        jnp.zeros((model_width,), jnp.float32),
        jnp.zeros((model_width,), jnp.float32),
    ]
    outputs = []
    input_grads = []
    for micro in range(batch_count):
        weights_now = (
            lax.all_gather(qkv_weight, ("dp", "seq"), axis=0, tiled=True),
            lax.all_gather(out_weight, ("dp", "seq"), axis=0, tiled=True),
            lax.all_gather(up_weight, ("dp", "seq"), axis=0, tiled=True),
            lax.all_gather(down_weight, ("dp", "seq"), axis=0, tiled=True),
            lax.all_gather(query_bias, ("dp", "seq"), axis=0, tiled=True),
            lax.all_gather(value_bias, ("dp", "seq"), axis=0, tiled=True),
            lax.all_gather(out_bias, ("dp", "seq"), axis=0, tiled=True),
            lax.all_gather(first_gain, ("dp", "seq"), axis=0, tiled=True),
            lax.all_gather(first_shift, ("dp", "seq"), axis=0, tiled=True),
            lax.all_gather(up_bias, ("dp", "seq"), axis=0, tiled=True),
            lax.all_gather(down_bias, ("dp", "seq"), axis=0, tiled=True),
            lax.all_gather(second_gain, ("dp", "seq"), axis=0, tiled=True),
            lax.all_gather(second_shift, ("dp", "seq"), axis=0, tiled=True),
        )
        (
            qkv_full,
            out_full,
            up_full,
            down_full,
            query_b,
            value_b,
            out_b,
            first_g,
            first_s,
            up_b,
            down_b,
            second_g,
            second_s,
        ) = weights_now
        inputs = tokens[micro]
        merged = jnp.dot(inputs, qkv_full, preferred_element_type=jnp.float32)
        query = (merged[:, :model_width] + query_b.astype(jnp.float32)).astype(jnp.bfloat16)
        keys_now = merged[:, model_width : 2 * model_width].astype(jnp.bfloat16)
        values_now = (merged[:, 2 * model_width :] + value_b.astype(jnp.float32)).astype(
            jnp.bfloat16
        )
        whole_keys = lax.all_gather(
            jnp.concatenate([keys_now, values_now], axis=1), "seq", axis=0, tiled=True
        )
        padded = jnp.pad(whole_keys, ((reach * row_count, reach * row_count), (0, 0)))
        picked = lax.dynamic_slice_in_dim(padded, position * row_count, window * row_count, 0)
        key_stack = picked.reshape(window, row_count, 2 * model_width)
        key_segments = lax.dynamic_slice_in_dim(
            padded_segment[micro], position * row_count, window * row_count, 0
        ).reshape(window, row_count)
        query_segment = segments[micro]
        query_heads = head_split(query)
        log_total = log_totals(query_heads, key_stack, key_segments, query_segment)
        attended_f, exact_heads = attend_values(
            query_heads, key_stack, key_segments, query_segment, log_total
        )
        attended = attended_f.astype(jnp.bfloat16)
        branch = jnp.dot(attended, out_full, preferred_element_type=jnp.float32) + out_b.astype(
            jnp.float32
        )
        hidden, first_pull = jax.vjp(
            norm_layer,
            inputs.astype(jnp.float32) + branch,
            first_g.astype(jnp.float32),
            first_s.astype(jnp.float32),
        )
        hidden_low = hidden.astype(jnp.bfloat16)
        inner_rows = jnp.dot(hidden_low, up_full, preferred_element_type=jnp.float32) + up_b.astype(
            jnp.float32
        )
        activated, gelu_pull = jax.vjp(exact_gelu, inner_rows)
        activated_low = activated.astype(jnp.bfloat16)
        second = jnp.dot(
            activated_low, down_full, preferred_element_type=jnp.float32
        ) + down_b.astype(jnp.float32)
        output, second_pull = jax.vjp(
            norm_layer, hidden + second, second_g.astype(jnp.float32), second_s.astype(jnp.float32)
        )
        outputs.append(output.astype(jnp.bfloat16))
        back_weights = (
            lax.all_gather(qkv_weight, ("dp", "seq"), axis=0, tiled=True),
            lax.all_gather(out_weight, ("dp", "seq"), axis=0, tiled=True),
            lax.all_gather(up_weight, ("dp", "seq"), axis=0, tiled=True),
            lax.all_gather(down_weight, ("dp", "seq"), axis=0, tiled=True),
            lax.all_gather(query_bias, ("dp", "seq"), axis=0, tiled=True),
            lax.all_gather(value_bias, ("dp", "seq"), axis=0, tiled=True),
            lax.all_gather(out_bias, ("dp", "seq"), axis=0, tiled=True),
            lax.all_gather(first_gain, ("dp", "seq"), axis=0, tiled=True),
            lax.all_gather(first_shift, ("dp", "seq"), axis=0, tiled=True),
            lax.all_gather(up_bias, ("dp", "seq"), axis=0, tiled=True),
            lax.all_gather(down_bias, ("dp", "seq"), axis=0, tiled=True),
            lax.all_gather(second_gain, ("dp", "seq"), axis=0, tiled=True),
            lax.all_gather(second_shift, ("dp", "seq"), axis=0, tiled=True),
        )
        qkv_full, out_full, up_full, down_full = (
            back_weights[0],
            back_weights[1],
            back_weights[2],
            back_weights[3],
        )
        grad_sum2, grad_gain2, grad_shift2 = second_pull(cotangent[micro].astype(jnp.float32))
        grad_second = grad_sum2.astype(jnp.bfloat16)
        (grad_inner_f,) = gelu_pull(data_grad(grad_second, down_full))
        grad_inner = grad_inner_f.astype(jnp.bfloat16)
        grad_hidden = grad_sum2 + data_grad(grad_inner, up_full)
        grad_sum1, grad_gain1, grad_shift1 = first_pull(grad_hidden)
        grad_branch = grad_sum1.astype(jnp.bfloat16)
        grad_attended = data_grad(grad_branch, out_full).astype(jnp.bfloat16)
        grad_query_f, contrib = attention_back(
            query_heads,
            head_split(grad_attended),
            key_stack,
            key_segments,
            query_segment,
            log_total,
            exact_heads,
        )
        block_ids = position - reach + jnp.arange(window, dtype=jnp.int32)
        inside = (block_ids >= 0) & (block_ids < seq_count)
        canvas = jnp.zeros((seq_count, row_count, 2 * model_width), jnp.float32)
        canvas = canvas.at[jnp.clip(block_ids, 0, seq_count - 1)].add(
            jnp.where(inside[:, None, None], contrib, 0.0)
        )
        canvas = canvas.reshape(seq_count * row_count, 2 * model_width)
        key_value_grad = lax.psum_scatter(canvas, "seq", scatter_dimension=0, tiled=True)
        grad_query = grad_query_f.astype(jnp.bfloat16)
        grad_value = key_value_grad[:, model_width:].astype(jnp.bfloat16)
        grad_merged = jnp.concatenate(
            [grad_query, key_value_grad[:, :model_width].astype(jnp.bfloat16), grad_value], axis=1
        )
        input_grads.append((grad_sum1 + data_grad(grad_merged, qkv_full)).astype(jnp.bfloat16))
        terms = [
            weight_grad(inputs, grad_merged),
            weight_grad(attended, grad_branch),
            weight_grad(hidden_low, grad_inner),
            weight_grad(activated_low, grad_second),
            column_sum(grad_query),
            column_sum(grad_value),
            column_sum(grad_branch),
            grad_gain1,
            grad_shift1,
            column_sum(grad_inner),
            column_sum(grad_second),
            grad_gain2,
            grad_shift2,
        ]
        totals = [total_item + term_item for total_item, term_item in zip(totals, terms)]
    scattered = (
        lax.psum_scatter(totals[0], ("dp", "seq"), scatter_dimension=0, tiled=True),
        lax.psum_scatter(totals[1], ("dp", "seq"), scatter_dimension=0, tiled=True),
        lax.psum_scatter(totals[2], ("dp", "seq"), scatter_dimension=0, tiled=True),
        lax.psum_scatter(totals[3], ("dp", "seq"), scatter_dimension=0, tiled=True),
        lax.psum_scatter(totals[4], ("dp", "seq"), scatter_dimension=0, tiled=True),
        lax.psum_scatter(totals[5], ("dp", "seq"), scatter_dimension=0, tiled=True),
        lax.psum_scatter(totals[6], ("dp", "seq"), scatter_dimension=0, tiled=True),
        lax.psum_scatter(totals[7], ("dp", "seq"), scatter_dimension=0, tiled=True),
        lax.psum_scatter(totals[8], ("dp", "seq"), scatter_dimension=0, tiled=True),
        lax.psum_scatter(totals[9], ("dp", "seq"), scatter_dimension=0, tiled=True),
        lax.psum_scatter(totals[10], ("dp", "seq"), scatter_dimension=0, tiled=True),
        lax.psum_scatter(totals[11], ("dp", "seq"), scatter_dimension=0, tiled=True),
        lax.psum_scatter(totals[12], ("dp", "seq"), scatter_dimension=0, tiled=True),
    )
    return (
        jnp.stack(outputs),
        jnp.stack(input_grads),
        scattered[0],
        scattered[1],
        scattered[2],
        scattered[3],
        scattered[4],
        scattered[5],
        scattered[6],
        scattered[7],
        scattered[8],
        scattered[9],
        scattered[10],
        scattered[11],
        scattered[12],
    )


CORE, XBIT, ZLOW, ZHIGH = 1, 2, 4, 8
GROUPS = 4
GROUP = HEADS // GROUPS * HEAD_DIM
QROWS = 256


def swap(value, bit):
    return lax.ppermute(value, "seq", [(i, i ^ bit) for i in range(16)])


def swap_rows(value):
    return lax.ppermute(value, "dp", [(0, 1), (1, 0)])


def pair(bit, own, other):
    return jnp.where(bit == 0, own, other), jnp.where(bit == 0, other, own)


def join(bit, own, other, axis):
    return jnp.stack(pair(bit, own, other), axis=axis)


def take(value, index, axis):
    return lax.dynamic_index_in_dim(value, index, axis, keepdims=False)


def head_lanes(head, width):
    return lax.broadcasted_iota(jnp.int32, (1, width), 1) // HEAD_DIM == head


def attend_kernel(q_ref, k_ref, v_ref, qseg_ref, kseg_ref, out_ref, log_ref, bias_ref):
    width = q_ref.shape[1]
    rows = q_ref.shape[0]
    query = q_ref[...] * jnp.asarray(0.125, jnp.bfloat16)
    bias_ref[...] = jnp.where(qseg_ref[...] == kseg_ref[...], 0.0, NEGATIVE)
    total = jnp.zeros((rows, width), jnp.float32)
    for head in range(width // HEAD_DIM):
        lanes = head_lanes(head, width)
        masked = jnp.where(lanes, query, jnp.zeros_like(query))
        scores = lax.dot_general(
            masked, k_ref[...], (((1,), (1,)), ((), ())), preferred_element_type=jnp.float32
        )
        scores = scores + bias_ref[...]
        top = jnp.max(scores, axis=1, keepdims=True)
        expon = jnp.exp(scores - top)
        norm = jnp.sum(expon, axis=1, keepdims=True)
        value = jnp.dot(
            expon.astype(jnp.bfloat16), v_ref[...], preferred_element_type=jnp.float32
        )
        log_rows = jnp.transpose(jnp.broadcast_to(top + jnp.log(norm), (rows, 128)))
        log_ref[head : head + 1, :] = log_rows[0:1]
        total = total + jnp.where(lanes, value / norm, 0.0)
    out_ref[...] = total.astype(jnp.bfloat16)


def attend_group(query, keys, values, qseg_column, kseg_row):
    rows, width = query.shape
    count = keys.shape[0]
    return pl.pallas_call(
        attend_kernel,
        grid=(rows // QROWS,),
        in_specs=[
            pl.BlockSpec((QROWS, width), lambda i: (i, 0)),
            pl.BlockSpec((count, width), lambda i: (0, 0)),
            pl.BlockSpec((count, width), lambda i: (0, 0)),
            pl.BlockSpec((QROWS, 1), lambda i: (i, 0)),
            pl.BlockSpec((1, count), lambda i: (0, 0)),
        ],
        out_specs=[
            pl.BlockSpec((QROWS, width), lambda i: (i, 0)),
            pl.BlockSpec((8, QROWS), lambda i: (0, i)),
        ],
        out_shape=[
            jax.ShapeDtypeStruct((rows, width), jnp.bfloat16),
            jax.ShapeDtypeStruct((8, rows), jnp.float32),
        ],
        scratch_shapes=[pltpu.VMEM((QROWS, count), jnp.float32)],
        cost_estimate=pl.CostEstimate(
            flops=4 * rows * count * 256 * (width // HEAD_DIM),
            bytes_accessed=4 * (rows + count) * width,
            transcendentals=rows * count * (width // HEAD_DIM),
        ),
        compiler_params=pltpu.CompilerParams(vmem_limit_bytes=60 * 1024 * 1024),
    )(query, keys, values, qseg_column, kseg_row)


def attend_back_kernel(
    q_ref, k_ref, v_ref, grad_ref, log_ref, qseg_ref, kseg_ref, dq_ref, dk_ref, dv_ref, bias_ref
):
    width = q_ref.shape[1]
    query = q_ref[...] * jnp.asarray(0.125, jnp.bfloat16)
    grad = grad_ref[...]
    bias_ref[...] = jnp.where(kseg_ref[...] == qseg_ref[...], 0.0, NEGATIVE)

    @pl.when(pl.program_id(0) == 0)
    def clear():
        dk_ref[...] = jnp.zeros_like(dk_ref)
        dv_ref[...] = jnp.zeros_like(dv_ref)

    total = jnp.zeros(query.shape, jnp.float32)
    for head in range(width // HEAD_DIM):
        lanes = head_lanes(head, width)
        query_now = jnp.where(lanes, query, jnp.zeros_like(query))
        grad_now = jnp.where(lanes, grad, jnp.zeros_like(grad))
        scores = lax.dot_general(
            k_ref[...], query_now, (((1,), (1,)), ((), ())), preferred_element_type=jnp.float32
        )
        prob = jnp.exp(scores + bias_ref[...] - log_ref[head : head + 1, :])
        grad_prob = lax.dot_general(
            v_ref[...], grad_now, (((1,), (1,)), ((), ())), preferred_element_type=jnp.float32
        )
        delta = jnp.sum(prob * grad_prob, axis=0, keepdims=True)
        grad_score = (prob * (grad_prob - delta)).astype(jnp.bfloat16)
        dv_ref[...] += jnp.dot(
            prob.astype(jnp.bfloat16), grad_now, preferred_element_type=jnp.float32
        )
        dk_ref[...] += jnp.dot(grad_score, query_now, preferred_element_type=jnp.float32)
        dq = lax.dot_general(
            grad_score, k_ref[...], (((0,), (0,)), ((), ())), preferred_element_type=jnp.float32
        )
        total = total + jnp.where(lanes, dq * 0.125, 0.0)
    dq_ref[...] = total.astype(jnp.bfloat16)


def attend_group_back(query, keys, values, grad, log_total, qseg_row, kseg_column):
    rows, width = query.shape
    count = keys.shape[0]
    return pl.pallas_call(
        attend_back_kernel,
        grid=(rows // QROWS,),
        in_specs=[
            pl.BlockSpec((QROWS, width), lambda i: (i, 0)),
            pl.BlockSpec((count, width), lambda i: (0, 0)),
            pl.BlockSpec((count, width), lambda i: (0, 0)),
            pl.BlockSpec((QROWS, width), lambda i: (i, 0)),
            pl.BlockSpec((8, QROWS), lambda i: (0, i)),
            pl.BlockSpec((1, QROWS), lambda i: (0, i)),
            pl.BlockSpec((count, 1), lambda i: (0, 0)),
        ],
        out_specs=[
            pl.BlockSpec((QROWS, width), lambda i: (i, 0)),
            pl.BlockSpec((count, width), lambda i: (0, 0)),
            pl.BlockSpec((count, width), lambda i: (0, 0)),
        ],
        out_shape=[
            jax.ShapeDtypeStruct((rows, width), jnp.bfloat16),
            jax.ShapeDtypeStruct((count, width), jnp.float32),
            jax.ShapeDtypeStruct((count, width), jnp.float32),
        ],
        scratch_shapes=[pltpu.VMEM((count, QROWS), jnp.float32)],
        cost_estimate=pl.CostEstimate(
            flops=10 * rows * count * 256 * (width // HEAD_DIM),
            bytes_accessed=8 * (rows + count) * width,
            transcendentals=rows * count * (width // HEAD_DIM),
        ),
        compiler_params=pltpu.CompilerParams(vmem_limit_bytes=60 * 1024 * 1024),
    )(query, keys, values, grad, log_total, qseg_row, kseg_column)


def norm_parts(summed):
    centred = summed - jnp.mean(summed, axis=-1, keepdims=True)
    scale = lax.rsqrt(jnp.mean(centred * centred, axis=-1, keepdims=True) + EPS)
    return centred * scale, scale


def norm_back(grad, normal, scale, gain):
    grad_normal = grad * gain
    inside = grad_normal - jnp.mean(grad_normal, axis=-1, keepdims=True)
    return scale * (inside - normal * jnp.mean(grad_normal * normal, axis=-1, keepdims=True))


def gather_tokens(tokens, seq_mine):
    first = jnp.concatenate(
        [take(tokens, seq_mine, 0), swap(take(tokens, 1 - seq_mine, 0), ZHIGH)]
    )
    half = tokens.shape[-1] // 2
    block = first.shape[0]
    left, right = first[:, :half], first[:, half:]
    left_two = jnp.concatenate([left, swap(left, XBIT)])
    right_z = swap(right, ZLOW)
    left_far = swap(left_two, ZLOW)
    right_far = swap(jnp.concatenate([right, right_z]), XBIT)
    right_four = jnp.concatenate([right, right_far[:block], right_z, right_far[block:]])
    return jnp.concatenate([jnp.concatenate([left_two, left_far]), right_four], axis=1)


def gather_segments(segments, seq_mine):
    held = jnp.concatenate(
        [take(segments, seq_mine, 0), swap(take(segments, 1 - seq_mine, 0), ZHIGH)]
    ).reshape(1, -1)
    held = jnp.concatenate([held, swap(held, XBIT)], axis=1)
    held = jnp.concatenate([held, swap(held, ZLOW)], axis=1)
    return jnp.concatenate([held, swap(held, CORE)], axis=1)


def add_pair(one, other):
    return one.astype(jnp.float32) + other.astype(jnp.float32)


def scatter_first(partial):
    block = partial.shape[0] // 4
    low = partial.astype(jnp.bfloat16)
    return (
        swap(low[3 * block :], XBIT | ZLOW),
        swap(low[block : 2 * block], XBIT),
        swap(low[2 * block : 3 * block], ZLOW),
    )


def scatter_second(partial, got):
    block = partial.shape[0] // 4
    total = partial[:block] + add_pair(got[0], got[1]) + got[2].astype(jnp.float32)
    mine = block // 2
    return total[:mine], swap(total[mine:].astype(jnp.bfloat16), ZHIGH)


def gather_group_weight(weight, query_bias, value_bias, place):
    dp_at, z_high, z_low, x_at, core = place
    rows = weight.shape[0]
    pieces = weight.reshape(rows, 3, 2, 2, GROUP).transpose(2, 3, 0, 1, 4)
    pieces = pieces.reshape(2, 2, rows, 3 * GROUP)
    biases = jnp.concatenate([query_bias, value_bias])
    extra = jnp.pad(biases[None], ((0, 7), (0, 3 * GROUP - biases.shape[0])))
    extra = jnp.broadcast_to(extra[None, None], (2, 2) + extra.shape)
    pieces = jnp.concatenate([pieces, extra], axis=2)
    held = join(x_at, take(pieces, x_at, 1), swap(take(pieces, 1 - x_at, 1), XBIT), 0)
    held = join(z_low, take(held, z_low, 1), swap(take(held, 1 - z_low, 1), ZLOW), 0)
    held = join(z_high, held, swap(held, ZHIGH), 0)
    held = join(dp_at, held, swap_rows(held), 0)
    held = join(core, held, swap(held, CORE), 4)
    held = held.reshape(32, rows + 8, 3 * GROUP)
    group = z_low * 2 + x_at
    query_full = held[:, rows, :rows].reshape(-1)
    value_full = held[:, rows, rows : 2 * rows].reshape(-1)
    return (
        held[:, :rows].reshape(32 * rows, 3 * GROUP),
        take(query_full.reshape(GROUPS, GROUP), group, 0),
        take(value_full.reshape(GROUPS, GROUP), group, 0),
    )


def swap_any(value, bits):
    return lax.ppermute(value, ("dp", "seq"), [(i, i ^ bits) for i in range(32)])


class GroupChain:
    def __init__(self, grad, query_sums, value_sums, place):
        dp_at, z_high, z_low, x_at, core = self.place = place
        self.rows = rows = grad.shape[0] // 32
        group = z_low * 2 + x_at
        sums = jnp.concatenate([query_sums.reshape(8, rows), value_sums.reshape(8, rows)], axis=1)
        owner = jnp.arange(32, dtype=jnp.int32)[:, None] // 8 == group
        sums = jnp.where(owner, jnp.tile(sums, (4, 1)), 0.0)
        extra = jnp.pad(sums[:, None], ((0, 0), (0, 7), (0, 3 * GROUP - 2 * rows)))
        held = jnp.concatenate([grad.reshape(32, rows, 3 * GROUP), extra], axis=1)
        self.shape = held.shape[1:]
        held = held.astype(jnp.bfloat16).reshape((2, 8, 2) + self.shape)

        def part(at_dp, at_core):
            return take(take(held, at_dp, 0), at_core, 1)

        self.kept = part(dp_at, core)
        self.got = [
            swap_any(part(1 - dp_at, 1 - core), 16 | CORE),
            swap_any(part(1 - dp_at, core), 16),
            swap_any(part(dp_at, 1 - core), CORE),
        ]

    def next(self):
        z_high = self.place[1]
        held = add_pair(self.kept, self.got[0]) + add_pair(self.got[1], self.got[2])
        held = held.astype(jnp.bfloat16).reshape((2, 4) + self.shape)
        self.kept = take(held, z_high, 0)
        self.got = swap(take(held, 1 - z_high, 0), ZHIGH)

    def last(self):
        _, _, z_low, x_at, _ = self.place
        held = add_pair(self.kept, self.got).astype(jnp.bfloat16)
        at = z_low * 2 + x_at
        self.kept = take(held, at, 0)
        self.got = [
            swap(take(held, at ^ other, 0), bits)
            for other, bits in ((3, XBIT | ZLOW), (2, ZLOW), (1, XBIT))
        ]

    def result(self):
        _, _, z_low, x_at, _ = self.place
        far, z_part, x_part = self.got
        near, other = pair(x_at, self.kept, x_part), pair(x_at, z_part, far)
        low, high = zip(*(pair(z_low, one, two) for one, two in zip(near, other)))
        held = jnp.stack(low + high).astype(jnp.float32)
        rows = self.rows
        weight = held[:, :rows].reshape(GROUPS, rows, 3, GROUP).transpose(1, 2, 0, 3)
        biases = jnp.sum(held[:, rows, : 2 * rows], axis=0)
        return weight.reshape(rows, 3 * GROUPS * GROUP), biases[:rows], biases[rows:]


class Chain:
    def __init__(self, held, place):
        self.place = place
        self.left = list(range(5))
        self.rows, self.columns = held.shape[1:]
        self.held = held.reshape(32 * self.rows, self.columns)

    def half(self, at):
        before = 2**self.axis
        split = self.held.reshape(before, 2, -1, self.columns)
        return take(split, at, 1).reshape(-1, self.columns)

    def send(self, step):
        self.step, self.axis = step, self.left.index(step)
        bits = (None, ZHIGH, ZLOW, XBIT, CORE)
        sent = self.half(1 - self.place[step])
        self.got = swap(sent, bits[step]) if step else swap_rows(sent)

    def add(self):
        self.left.remove(self.step)
        kept = self.half(self.place[self.step]).astype(jnp.float32)
        kept = kept + self.got.astype(jnp.float32)
        self.held = kept.astype(jnp.bfloat16) if self.left else kept


def meet(values, chains):
    values, got = lax.optimization_barrier((values, [chain.got for chain in chains]))
    for chain, arrived in zip(chains, got):
        chain.got = arrived
        chain.add()
    return values


def heads_to_owners(attended, place):
    _, _, z_low, x_at, _ = place
    block = attended.shape[0] // 4
    own = attended[:block]
    x_part = swap(attended[block : 2 * block], XBIT)
    z_part = swap(attended[2 * block : 3 * block], ZLOW)
    far_part = swap(attended[3 * block :], XBIT | ZLOW)
    near = jnp.concatenate(pair(x_at, own, x_part), axis=1)
    far = jnp.concatenate(pair(x_at, z_part, far_part), axis=1)
    rows = jnp.concatenate(pair(z_low, near, far), axis=1)
    mine = block // 2
    return jnp.concatenate([rows[:mine], swap(rows[mine:], ZHIGH)])


def owners_to_rows(rows):
    mine = rows.shape[0] // 2
    return jnp.concatenate([rows[:mine], swap(rows[mine:], ZHIGH)])


def rows_to_heads(rows, place):
    _, _, z_low, x_at, _ = place
    near, far = pair(z_low, rows[:, : 2 * GROUP], rows[:, 2 * GROUP :])
    own, x_part = pair(x_at, near[:, :GROUP], near[:, GROUP:])
    z_part, far_part = pair(x_at, far[:, :GROUP], far[:, GROUP:])
    return jnp.concatenate(
        [own, swap(x_part, XBIT), swap(z_part, ZLOW), swap(far_part, XBIT | ZLOW)]
    )


def local(
    tokens,
    segments,
    qkv_weight,
    out_weight,
    up_weight,
    down_weight,
    query_bias,
    value_bias,
    out_bias,
    first_gain,
    first_shift,
    up_bias,
    down_bias,
    second_gain,
    second_shift,
    cotangent,
):
    f32, low = jnp.float32, jnp.bfloat16
    width = tokens.shape[-1]
    shard = out_weight.shape[0]
    up_chunks = up_weight.shape[1] // width
    wide = up_chunks * shard
    vectors = (out_bias, first_gain, first_shift, down_bias, second_gain, second_shift)
    position = lax.axis_index("seq")
    z_high, z_low = position // 8, position // 4 % 2
    x_at, core = position // 2 % 2, position % 2
    place = (lax.axis_index("dp"), z_high, z_low, x_at, core)
    mine = z_high

    up_parts = up_weight.reshape(shard, up_chunks, width).transpose(1, 0, 2).reshape(wide, width)
    small, start = jnp.zeros((8, width), low), 0
    for vector in vectors + (up_bias,):
        ends = (start, width - start - vector.shape[0])
        small, start = small + jnp.pad(vector[None], ((0, 7), ends)), start + vector.shape[0]
    packed = jnp.concatenate([out_weight, up_parts, down_weight, small])
    gathered = lax.all_gather(packed, ("dp", "seq"), axis=0)

    group_tokens = gather_tokens(tokens, mine)
    all_segments = gather_segments(segments, mine)
    group_weight, query_b, value_b = gather_group_weight(
        qkv_weight, query_bias, value_bias, place
    )
    half = group_tokens.shape[0]
    query = jnp.dot(group_tokens, group_weight[:, :GROUP], preferred_element_type=f32)
    query = (query + query_b.astype(f32)).astype(low)
    key_value = jnp.dot(group_tokens, group_weight[:, GROUP:], preferred_element_type=f32)
    lift = jnp.concatenate([jnp.zeros((GROUP,), f32), value_b.astype(f32)])
    key_value = (key_value + lift).astype(low)
    key_value = jnp.concatenate([key_value, swap(key_value, CORE)])
    keys, values = key_value[:, :GROUP], key_value[:, GROUP:]
    segment_column = all_segments.reshape(-1, 1)
    attended_group, log_total = attend_group(
        query, keys, values, segment_column[:half], all_segments
    )
    attended = heads_to_owners(attended_group, place)

    out_full = gathered[:, :shard].reshape(-1, width)
    up_full = jnp.concatenate(
        [
            gathered[:, shard * (1 + at) : shard * (2 + at)].reshape(-1, width)
            for at in range(up_chunks)
        ],
        axis=1,
    )
    down_full = gathered[:, shard + wide : shard + 2 * wide].reshape(-1, width)
    flat = gathered[:, shard + 2 * wide].astype(f32)
    count_small = len(vectors)
    rows_small = flat[:, : count_small * shard].reshape(32, count_small, shard)
    rows_small = rows_small.transpose(1, 0, 2).reshape(count_small, width)
    out_b, first_g, first_s, down_b, second_g, second_s = (
        rows_small[at : at + 1] for at in range(count_small)
    )
    up_b = flat[:, 6 * shard : 6 * shard + wide].reshape(-1)

    attended, up_full, down_full = lax.optimization_barrier((attended, up_full, down_full))
    inputs = jnp.concatenate([take(tokens, mine, 0), take(tokens, 1 - mine, 0)])
    branch = jnp.dot(attended, out_full, preferred_element_type=f32) + out_b
    normal1, scale1 = norm_parts(inputs.astype(f32) + branch)
    hidden = normal1 * first_g + first_s
    hidden_low = hidden.astype(low)
    inner = jnp.dot(hidden_low, up_full, preferred_element_type=f32) + up_b
    activated, gelu_pull = jax.vjp(exact_gelu, inner)
    activated_low = activated.astype(low)
    second = jnp.dot(activated_low, down_full, preferred_element_type=f32) + down_b
    normal2, scale2 = norm_parts(hidden + second)
    output = (normal2 * second_g + second_s).astype(low)
    output = jnp.stack(pair(mine, output[: output.shape[0] // 2], output[output.shape[0] // 2 :]))

    upstream = jnp.concatenate([take(cotangent, mine, 0), take(cotangent, 1 - mine, 0)])
    upstream = upstream.astype(f32)
    grad_sum2 = norm_back(upstream, normal2, scale2, second_g)
    grad_second = grad_sum2.astype(low)
    (grad_inner,) = gelu_pull(data_grad(grad_second, down_full))
    grad_inner = grad_inner.astype(low)
    grad_hidden = grad_sum2 + data_grad(grad_inner, up_full)
    grad_sum1 = norm_back(grad_hidden, normal1, scale1, first_g)
    grad_branch = grad_sum1.astype(low)
    grad_attended = data_grad(grad_branch, out_full).astype(low)
    grad_rows = owners_to_rows(grad_attended)
    _, activated_low = lax.optimization_barrier((grad_attended, activated_low))
    grad_rows, hidden_low, attended = lax.optimization_barrier((grad_rows, hidden_low, attended))

    grad_down = weight_grad(activated_low, grad_second).astype(low)
    grad_up = weight_grad(hidden_low, grad_inner).astype(low)
    grad_out = weight_grad(attended, grad_branch).astype(low)
    sums = (
        column_sum(grad_branch),
        jnp.sum(grad_hidden * normal1, axis=0),
        jnp.sum(grad_hidden, axis=0),
        column_sum(grad_second),
        jnp.sum(upstream * normal2, axis=0),
        jnp.sum(upstream, axis=0),
    )
    sums = jnp.stack(sums).reshape(len(sums), 32, shard).transpose(1, 0, 2).reshape(32, -1)
    sums = jnp.concatenate([sums, column_sum(grad_inner).reshape(32, wide)], axis=1)
    sums = jnp.pad(sums[:, None], ((0, 0), (0, 7), (0, width - sums.shape[1]))).astype(low)
    rest = jnp.concatenate([grad_out.reshape(32, shard, width), sums], axis=1)
    at_dp, at_high, at_low, at_x, at_core = range(5)
    down = Chain(grad_down.reshape(32, wide, width), place)
    up = Chain(grad_up.reshape(32, shard, -1), place)
    rest = Chain(rest, place)
    chains = (down, up, rest)
    for chain in chains:
        chain.send(at_core)

    grad_group = rows_to_heads(grad_rows, place)
    grad_group = meet(grad_group, chains)
    down.send(at_x)
    up.send(at_dp)
    rest.send(at_high)
    attention = attend_group_back(
        query, keys, values, grad_group, log_total, all_segments[:, :half], segment_column
    )
    grad_query, grad_keys, grad_values = meet(attention, chains)
    down.send(at_dp)
    up.send(at_x)
    rest.send(at_dp)
    grad_kv = jnp.concatenate([grad_keys, grad_values], axis=1)
    grad_kv = grad_kv[:half] + swap(grad_kv[half:].astype(low), CORE).astype(f32)
    grad_merged = jnp.concatenate([grad_query, grad_kv.astype(low)], axis=1)
    back = data_grad(grad_merged, group_weight)
    back_got = scatter_first(back)
    group_chain = GroupChain(
        weight_grad(group_tokens, grad_merged),
        column_sum(grad_merged[:, :GROUP]),
        column_sum(grad_merged[:, 2 * GROUP :]),
        place,
    )
    back_got, group_chain.got = meet((back_got, group_chain.got), chains)
    own_part, other_part = scatter_second(back, back_got)
    group_chain.next()
    down.send(at_low)
    up.send(at_high)
    rest.send(at_low)
    other_part, group_chain.got = meet((other_part, group_chain.got), chains)
    group_chain.last()
    down.send(at_high)
    up.send(at_low)
    rest.send(at_x)
    group_chain.got = meet(group_chain.got, chains)
    down_mine, up_mine, rest_mine = (chain.held for chain in chains)
    other_part = other_part.astype(f32)
    count = own_part.shape[0]
    own_grad = (grad_sum1[:count] + own_part).astype(low)
    other_grad = (grad_sum1[count:] + other_part).astype(low)
    input_grad = jnp.stack(pair(mine, own_grad, other_grad))
    grad_qkv, grad_query_bias, grad_value_bias = group_chain.result()

    tail = rest_mine[shard]
    parts = [tail[at * shard : (at + 1) * shard] for at in range(6)]
    return (
        output,
        input_grad,
        grad_qkv,
        rest_mine[:shard],
        up_mine,
        down_mine,
        grad_query_bias,
        grad_value_bias,
        parts[0],
        parts[1],
        parts[2],
        tail[6 * shard : 6 * shard + wide],
        parts[3],
        parts[4],
        parts[5],
    )


def solution(mesh):
    in_specs = (
        P("dp", "seq", None),
        P("dp", "seq"),
        P(("dp", "seq"), None),
        P(("dp", "seq"), None),
        P(("dp", "seq"), None),
        P(("dp", "seq"), None),
        P(("dp", "seq")),
        P(("dp", "seq")),
        P(("dp", "seq")),
        P(("dp", "seq")),
        P(("dp", "seq")),
        P(("dp", "seq")),
        P(("dp", "seq")),
        P(("dp", "seq")),
        P(("dp", "seq")),
        P("dp", "seq", None),
    )
    out_specs = (
        P("dp", "seq", None),
        P("dp", "seq", None),
        P(("dp", "seq"), None),
        P(("dp", "seq"), None),
        P(("dp", "seq"), None),
        P(("dp", "seq"), None),
        P(("dp", "seq")),
        P(("dp", "seq")),
        P(("dp", "seq")),
        P(("dp", "seq")),
        P(("dp", "seq")),
        P(("dp", "seq")),
        P(("dp", "seq")),
        P(("dp", "seq")),
        P(("dp", "seq")),
    )
    fits = mesh.shape["dp"] == 2 and mesh.shape["seq"] == 16
    return jax.shard_map(
        local if fits else general_local, mesh=mesh, in_specs=in_specs, out_specs=out_specs, check_vma=False
    )
```
